128 devices in a mesh: row: 16 (over z, x), col: 8 (over y, core).
Axes of the slice: x: 4, y: 4, z: 4, core: 2. Of those that a mesh axis runs over, the one named last changes fastest.
Arguments:
- cam_jac: float32 [512, 18, 512], P(('row', 'col')), may hold values from -1 to 1
- land_jac: float32 [512, 6, 512], P(('row', 'col')), may hold values from -5 to 5
- resid: float32 [512, 2, 512], P(('row', 'col')), may hold values from -20 to 20
- obs_cam: int32 [512, 512], P(('row', 'col')), may hold values from 0 to 127
- obs_land: int32 [512, 512], P(('row', 'col')), may hold values from 0 to 127
- pairs: int32 [512, 2], P(('row', 'col')), may hold values from 0 to 31, as said below
- cam_damp: float32 [18432], P(('row', 'col')), may hold values from 1 to 10
Outputs:
- cam_step: float32 [18432], P(('row', 'col'))
- land_step: float32 [512, 3, 128], P(('row', 'col'))
The draws below stay inside these ranges and needn't reach their ends.
Inputs may be any that keep to these rules, and one draw needn't show every extreme that they name: `pairs`: clusters are laid out device by device, 4 a device, devices in order of row, then col. A cluster held at grid row r and grid column c is seen by a first group in [r * 2, (r + 1) * 2) and a different second group in [c * 4, (c + 1) * 4).
All inputs are finite; a program needn't handle non-finite values.
Results may differ from the reference program's by a relative error of at most 0.0003.
Values sent between devices are 32-bit elements; how exact they have to be, the bound alone decides.
A program may use at most 384 MiB of HBM per device.

```python
import math
import jax
import jax.numpy as jnp
from jax import lax

G = 32
CAM = 64
LM = 128
CL_DEV = 4
ITERS = 2
GW = 576
NS = 18432
OBS = 512
CL = 512
GROW = 2
GCOL = 4


def draw_pairs(key, part):
    cluster = jnp.arange(CL, dtype=jnp.int32)
    cols_count = G // GCOL
    grid_row = cluster // (CL_DEV * cols_count)
    grid_col = cluster // CL_DEV % cols_count
    key_first, key_free, key_skip = jax.random.split(key, 3)
    first = grid_row * GROW + jax.random.randint(key_first, (CL,), 0, GROW, dtype=jnp.int32)
    free_pick = jax.random.randint(key_free, (CL,), 0, GCOL, dtype=jnp.int32)
    skip_pick = jax.random.randint(key_skip, (CL,), 0, GCOL - 1, dtype=jnp.int32)
    within = first - grid_col * GCOL
    inside = (within >= 0) & (within < GCOL)
    skip_pick = skip_pick + (skip_pick >= within).astype(jnp.int32)
    second = grid_col * GCOL + jnp.where(inside, skip_pick, free_pick)
    return jnp.stack([first, second], axis=1).astype(jnp.int32)


def observe_indices(key):
    base_key = jax.random.fold_in(key, 101)
    key_landmark, key_offset = jax.random.split(base_key)
    landmark = jax.random.randint(key_landmark, (CL, OBS), 0, LM, dtype=jnp.int32)
    offset = jax.random.randint(key_offset, (CL, OBS), -3, 4, dtype=jnp.int32)
    center = landmark * (2 * CAM) // LM
    position = (center + offset) % (2 * CAM)
    camera = position % 2 * CAM + position // 2
    return (camera.astype(jnp.int32), landmark.astype(jnp.int32))


def signed_uniform(key, shape, lower, upper):
    key_signs, key_sizes = jax.random.split(key)
    signs = (jax.random.randint(key_signs, shape, 0, 2, dtype=jnp.int32) * 2 - 1).astype(jnp.float32)
    return signs * jax.random.uniform(key_sizes, shape, jnp.float32, lower, upper)


def cluster_floats(key):
    camera, landmark = observe_indices(key)
    subkeys = jax.random.split(jax.random.fold_in(key, 202), 9)
    cam_noise = jax.random.normal(subkeys[0], (CL, 18, OBS), jnp.float32)
    land_noise = jax.random.normal(subkeys[1], (CL, 6, OBS), jnp.float32)
    obs_noise = jax.random.normal(subkeys[2], (CL, 2, OBS), jnp.float32)
    amplitude = jax.random.uniform(subkeys[3], (CL, 9, 1), jnp.float32, 0.5, 1.5)
    cam_base = signed_uniform(subkeys[4], (CL, 18, 1), 0.2, 0.4)
    cam_jac = jnp.clip(cam_base + 0.06 * cam_noise, -1.0, 1.0)
    land_base = signed_uniform(subkeys[5], (CL, 6, 1), 1.5, 3.0)
    land_jac = jnp.clip(land_base + 0.3 * land_noise, -5.0, 5.0)
    angle_shift = jax.random.uniform(subkeys[6], (CL, 9, 1), jnp.float32, -math.pi, math.pi)
    place = (camera % CAM).astype(jnp.float32)[:, None, :]
    smooth_error = amplitude * jnp.cos(2.0 * math.pi * place / CAM + angle_shift)
    rough_table = 0.3 * jax.random.normal(subkeys[7], (CL, 9, 2 * CAM), jnp.float32)
    rough_error = jnp.take_along_axis(rough_table, jnp.broadcast_to(camera[:, None, :], (CL, 9, OBS)), axis=2)
    camera_error = smooth_error + rough_error
    point_table = 0.5 * jax.random.normal(subkeys[8], (CL, 3, LM), jnp.float32)
    point_error = jnp.take_along_axis(point_table, jnp.broadcast_to(landmark[:, None, :], (CL, 3, OBS)), axis=2)
    residual_rows = []
    for row_index in range(2):
        total_value = 0.3 * obs_noise[:, row_index]
        for param_index in range(9):
            total_value = total_value + cam_jac[:, row_index * 9 + param_index] * camera_error[:, param_index]
        for point_index in range(3):
            total_value = total_value + land_jac[:, row_index * 3 + point_index] * point_error[:, point_index]
        residual_rows.append(total_value)
    resid = jnp.clip(jnp.stack(residual_rows, axis=1), -20.0, 20.0)
    return (cam_jac, land_jac, resid)


def draw_obs_cam(key, part):
    return observe_indices(key)[0]


def draw_obs_land(key, part):
    return observe_indices(key)[1]


def draw_cam_jac(key, part):
    return cluster_floats(key)[0]


def draw_land_jac(key, part):
    return cluster_floats(key)[1]


def draw_resid(key, part):
    return cluster_floats(key)[2]


def levels(own_key, extent, cuts, least, top_value):
    def one(dim, parts):
        steps = jax.random.uniform(jax.random.fold_in(jax.random.fold_in(own_key, 6), dim), (parts,), jnp.float32, least / len(cuts), top_value / len(cuts))
        return jnp.repeat(jnp.exp(steps), extent[dim] // parts).reshape((-1,) + (1,) * (len(extent) - dim - 1))

    level = one(*cuts[0])
    for cut in cuts[1:]:
        level = level * one(*cut)
    return level


def setup_inputs(seed: int = 0) -> dict:
    streams_of = jax.random.split(jax.random.key(seed), 8)
    return {
        "cam_jac": draw_cam_jac(jax.random.fold_in(streams_of[7], 71), 0),
        "land_jac": draw_land_jac(jax.random.fold_in(streams_of[7], 71), 0),
        "resid": draw_resid(jax.random.fold_in(streams_of[7], 71), 0),
        "obs_cam": draw_obs_cam(jax.random.fold_in(streams_of[7], 71), 0),
        "obs_land": draw_obs_land(jax.random.fold_in(streams_of[7], 71), 0),
        "pairs": draw_pairs(jax.random.fold_in(streams_of[7], 71), 0),
        "cam_damp": jnp.clip(jnp.exp(math.log(10.0) - 2.3025851 * jax.random.uniform(streams_of[6], (NS,), jnp.float32) ** levels(streams_of[6], (NS,), ((0, 128),), -0.2, 0.2)), 1.0, 10.0),
    }


DAMPING = 1.0
HIGHEST = lax.Precision.HIGHEST

def cholesky_three(normal):
    root_first = jnp.sqrt(normal[0])
    inv_first = 1.0 / root_first
    low_one = normal[1] * inv_first
    low_two = normal[2] * inv_first
    inv_second = 1.0 / jnp.sqrt(normal[4] - low_one * low_one)
    low_three = (normal[5] - low_two * low_one) * inv_second
    inv_third = 1.0 / jnp.sqrt(normal[8] - low_two * low_two - low_three * low_three)
    return jnp.stack([inv_first, low_one, low_two, inv_second, low_three, inv_third])

def lower_solve(factor, first, second, third):
    out_one = first * factor[0]
    out_two = (second - factor[1] * out_one) * factor[3]
    out_three = (third - factor[2] * out_one - factor[4] * out_two) * factor[5]
    return jnp.stack([out_one, out_two, out_three])

def upper_solve(factor, first, second, third):
    out_three = third * factor[5]
    out_two = (second - factor[4] * out_three) * factor[3]
    out_one = (first - factor[1] * out_two - factor[2] * out_three) * factor[0]
    return jnp.stack([out_one, out_two, out_three])

def cluster_schur(cam_jac, land_jac, resid, obs_cam, obs_land):
    count = obs_cam.shape[0]
    width = CAM * 9
    cam_rows = cam_jac.reshape(2, 9, count)
    land_rows = land_jac.reshape(2, 3, count)
    coupled = cam_rows[0][:, None, :] * land_rows[0][None] + cam_rows[1][:, None, :] * land_rows[1][None]
    land_outer = (land_rows[0][:, None, :] * land_rows[0][None] + land_rows[1][:, None, :] * land_rows[1][None]).reshape(9, count)
    cam_outer = (cam_rows[0][:, None, :] * cam_rows[0][None] + cam_rows[1][:, None, :] * cam_rows[1][None]).reshape(81, count)
    cam_grad = cam_rows[0] * resid[0] + cam_rows[1] * resid[1]
    land_grad = land_rows[0] * resid[0] + land_rows[1] * resid[1]
    land_onehot = (obs_land[None, :] == jnp.arange(LM, dtype=jnp.int32)[:, None]).astype(jnp.float32)
    cam_onehot = (obs_cam[None, :] == jnp.arange(2 * CAM, dtype=jnp.int32)[:, None]).astype(jnp.float32)
    land_normal = jnp.dot(land_outer, land_onehot.T, precision=HIGHEST) + DAMPING * jnp.eye(3, dtype=jnp.float32).reshape(9, 1)
    land_total = jnp.dot(land_grad, land_onehot.T, precision=HIGHEST)
    cam_normal = jnp.dot(cam_outer, cam_onehot.T, precision=HIGHEST)
    cam_total = jnp.dot(cam_grad, cam_onehot.T, precision=HIGHEST)
    factor = cholesky_three(land_normal)
    obs_factor = jnp.take(factor, obs_land, axis=1)
    solved = jnp.stack([lower_solve(obs_factor, coupled[param, 0], coupled[param, 1], coupled[param, 2]) for param in range(9)])
    row_index = obs_cam[None, None, :] * 9 + jnp.arange(9, dtype=jnp.int32)[:, None, None]
    col_index = jnp.arange(3, dtype=jnp.int32)[None, :, None] * LM + obs_land[None, None, :]
    coupling = jnp.zeros((2 * width, 3 * LM), jnp.float32).at[row_index, col_index].add(solved)
    tvector = lower_solve(factor, land_total[0], land_total[1], land_total[2]).reshape(3 * LM)
    blocks = cam_normal.T.reshape(2, CAM, 9, 9)
    eye_cam = jnp.eye(CAM, dtype=jnp.float32)
    upper_first = (eye_cam[:, None, :, None] * blocks[0][:, :, None, :]).reshape(width, width)
    upper_second = (eye_cam[:, None, :, None] * blocks[1][:, :, None, :]).reshape(width, width)
    coupling_first = coupling[:width]
    coupling_second = coupling[width:]
    diag_first = upper_first - jnp.dot(coupling_first, coupling_first.T, precision=HIGHEST)
    cross = -jnp.dot(coupling_first, coupling_second.T, precision=HIGHEST)
    diag_second = upper_second - jnp.dot(coupling_second, coupling_second.T, precision=HIGHEST)
    right = -cam_total.T.reshape(2 * width) + jnp.dot(coupling, tvector, precision=HIGHEST)
    return (diag_first, cross, diag_second, right[:width], right[width:], coupling, tvector, factor)

def reference(cam_jac, land_jac, resid, obs_cam, obs_land, pairs, cam_damp):
    width = GW

    def accumulate(carry, items):
        diag_blocks, right_groups = carry
        jac_cam, jac_land, residual, cams, lands, pair = items
        diag_first, cross, diag_second, right_first, right_second, coupling, tvector, factor = cluster_schur(jac_cam, jac_land, residual, cams, lands)
        diag_blocks = diag_blocks.at[pair[0]].add(diag_first).at[pair[1]].add(diag_second)
        right_groups = right_groups.at[pair[0]].add(right_first).at[pair[1]].add(right_second)
        return ((diag_blocks, right_groups), cross)
    start = (jnp.zeros((G, width, width), jnp.float32), jnp.zeros((G, width), jnp.float32))
    (diag_blocks, right_groups), cross_blocks = lax.scan(accumulate, start, (cam_jac, land_jac, resid, obs_cam, obs_land, pairs))
    precond = 1.0 / (jnp.diagonal(diag_blocks, axis1=1, axis2=2).reshape(NS) + cam_damp)

    def apply_system(vector):
        groups = vector.reshape(G, width)
        image = jnp.einsum('gij,gj->gi', diag_blocks, groups, precision=HIGHEST)

        def add_pair(total, items):
            block, pair = items
            total = total.at[pair[0]].add(jnp.dot(block, groups[pair[1]], precision=HIGHEST))
            total = total.at[pair[1]].add(jnp.dot(groups[pair[0]], block, precision=HIGHEST))
            return (total, None)
        image, unused = lax.scan(add_pair, image, (cross_blocks, pairs))
        return image.reshape(NS) + cam_damp * vector
    solution = jnp.zeros((NS,), jnp.float32)
    residual = right_groups.reshape(NS)
    precon_res = precond * residual
    direction = precon_res
    norm_now = jnp.sum(residual * precon_res)
    for step in range(ITERS):
        image = apply_system(direction)
        alpha = norm_now / jnp.sum(direction * image)
        solution = solution + alpha * direction
        residual = residual - alpha * image
        if step + 1 < ITERS:
            precon_res = precond * residual
            norm_next = jnp.sum(residual * precon_res)
            direction = precon_res + norm_next / norm_now * direction
            norm_now = norm_next

    def landmark(items):
        jac_cam, jac_land, residual_obs, cams, lands, pair = items
        outputs = cluster_schur(jac_cam, jac_land, residual_obs, cams, lands)
        coupling, tvector, factor = (outputs[5], outputs[6], outputs[7])
        first_part = lax.dynamic_slice_in_dim(solution, (pair[0] * width).astype(jnp.int32), width)
        second_part = lax.dynamic_slice_in_dim(solution, (pair[1] * width).astype(jnp.int32), width)
        camera_part = jnp.concatenate([first_part, second_part])
        summed = (tvector + jnp.dot(camera_part, coupling, precision=HIGHEST)).reshape(3, LM)
        return -upper_solve(factor, summed[0], summed[1], summed[2])
    land_step = lax.map(landmark, (cam_jac, land_jac, resid, obs_cam, obs_land, pairs))
    return (solution, land_step)
```

```python
import jax
import jax.numpy as jnp
from jax import lax
from jax.experimental import pallas as pl
from jax.experimental.pallas import tpu as pltpu
from jax.sharding import PartitionSpec as P

DAMPING = 1.0
MESH = pl.DeviceIdType.MESH
LANES = 128


def lane_gather(table, index):
    rows = table.shape[0]
    dims = lax.GatherDimensionNumbers(
        offset_dims=(),
        collapsed_slice_dims=(1,),
        start_index_map=(1,),
        operand_batching_dims=(0,),
        start_indices_batching_dims=(0,),
    )
    pieces = []
    for at in range(0, index.shape[1], LANES):
        piece = jnp.broadcast_to(index[:, at : at + LANES], (rows, LANES))
        pieces.append(
            lax.gather(
                table,
                piece[..., None],
                dims,
                slice_sizes=(1, 1),
                mode=lax.GatherScatterMode.PROMISE_IN_BOUNDS,
            )
        )
    return pieces[0] if len(pieces) == 1 else jnp.concatenate(pieces, axis=1)


def exact_dot(x, onehot):
    rows = x.shape[0]
    high = x.astype(jnp.bfloat16)
    rest = x - high.astype(jnp.float32)
    mid = rest.astype(jnp.bfloat16)
    low = (rest - mid.astype(jnp.float32)).astype(jnp.bfloat16)
    stacked = jnp.concatenate([high, mid, low], axis=0)
    out = jnp.dot(stacked, onehot, preferred_element_type=jnp.float32)
    return out[:rows] + (out[rows : 2 * rows] + out[2 * rows :])


def rows_of(pieces, rows):
    have = sum(p.shape[0] for p in pieces)
    if have < rows:
        pieces = list(pieces) + [jnp.zeros((rows - have, pieces[0].shape[1]), jnp.float32)]
    return jnp.concatenate(pieces, axis=0)


def col_sum(x):
    return jnp.sum(x, axis=0, keepdims=True)


def lower_solve(f, a, b, c):
    one = a * f[0]
    two = (b - f[1] * one) * f[3]
    three = (c - f[2] * one - f[4] * two) * f[5]
    return one, two, three


def upper_solve(f, a, b, c):
    three = c * f[5]
    two = (b - f[4] * three) * f[3]
    one = (a - f[1] * two - f[2] * three) * f[0]
    return one, two, three


def normal_solve(f, a, b, c):
    return upper_solve(f, *lower_solve(f, a, b, c))


def cholesky_three(v):
    inv_first = 1.0 / jnp.sqrt(v[0])
    low_one = v[1] * inv_first
    low_two = v[2] * inv_first
    inv_second = 1.0 / jnp.sqrt(v[3] - low_one * low_one)
    low_three = (v[4] - low_two * low_one) * inv_second
    inv_third = 1.0 / jnp.sqrt(v[5] - low_two * low_two - low_three * low_three)
    return inv_first, low_one, low_two, inv_second, low_three, inv_third


def make_kernel(n_row, n_col, n_cl, n_obs):
    f32 = jnp.float32

    def kernel(
        pairs_ref, cj_ref, lj_ref, re_ref, oc_ref, ol_ref, damp_ref,
        cam_ref, land_ref,
        jac, one_cam, one_land, fac, yvec, msg1, msg2, sums,
        in1, in2, zbuf, tbuf, sc1, sc2, stot,
        s1, r1, s2, r2, s3, r3, s4, r4, s5, r5, s6, r6,
    ):
        row = lax.axis_index("row")
        col = lax.axis_index("col")
        hub_col = row // 2
        is_hub = col == hub_col
        up = lambda i: lax.rem(row + i, n_row)
        over = lambda i: lax.rem(col + i, n_col)

        barrier = pltpu.get_barrier_semaphore()
        for i in range(1, n_row):
            pl.semaphore_signal(barrier, inc=1, device_id=(up(i), col), device_id_type=MESH)
        for i in range(1, n_col):
            pl.semaphore_signal(barrier, inc=1, device_id=(row, over(i)), device_id_type=MESH)

        lane = lax.broadcasted_iota(jnp.int32, (16, LANES), 1)
        sub = lax.broadcasted_iota(jnp.int32, (16, LANES), 0)
        left = lane < 64

        flat = (lane - 16 * col) * 9 + sub
        mine = (lane >= 16 * col) & (lane < 16 * col + 16) & (sub < 9)
        flat = jnp.where(mine, flat, 0)
        damp_low = jnp.broadcast_to(damp_ref[:, :LANES], (16, LANES))
        damp_high = jnp.broadcast_to(
            jnp.concatenate([damp_ref[:, LANES:], jnp.zeros((1, 2 * LANES - 144), f32)], axis=1),
            (16, LANES),
        )

        def gather_rows(table, index):
            dims = lax.GatherDimensionNumbers((), (1,), (1,), (0,), (0,))
            return lax.gather(
                table, index[..., None], dims, slice_sizes=(1, 1),
                mode=lax.GatherScatterMode.PROMISE_IN_BOUNDS,
            )

        damp = jnp.where(
            flat < LANES,
            gather_rows(damp_low, jnp.minimum(flat, LANES - 1)),
            gather_rows(damp_high, jnp.maximum(flat - LANES, 0)),
        )
        damp = jnp.where(mine, damp, 0.0)

        first = [pairs_ref[k, 0] - 2 * row for k in range(n_cl)]
        second = [pairs_ref[k, 1] - 4 * col for k in range(n_cl)]

        def place(tiles, out, k):
            rolled = pltpu.roll(out, 64, axis=1)
            half = lax.broadcasted_iota(jnp.int32, out.shape, 1) < 64

            def pick(cond, x):
                return jnp.where(cond, x, 0.0)

            a, b = first[k], second[k]
            return (
                tiles[0] + jnp.where(half, pick(a == 0, out), pick(a == 1, rolled)),
                tiles[1] + jnp.where(half, pick(b == 0, rolled), pick(b == 1, out)),
                tiles[2] + jnp.where(half, pick(b == 2, rolled), pick(b == 3, out)),
            )

        def vector_of(tiles, k):
            a, b = first[k], second[k]
            own = jnp.where(a == 0, tiles[0], pltpu.roll(tiles[0], 64, axis=1))
            other = jnp.where(b < 2, tiles[1], tiles[2])
            other = jnp.where((b == 1) | (b == 3), other, pltpu.roll(other, 64, axis=1))
            return jnp.where(left, own, other)

        keys = oc_ref[...] * LANES + ol_ref[...]
        keys_f = jnp.concatenate([keys.astype(f32), jnp.zeros((8 - n_cl, n_obs), f32)], axis=0)
        keys_t = keys_f.T
        cam_iota = lax.broadcasted_iota(jnp.int32, (LANES, n_obs), 0)
        zero = jnp.zeros((32, LANES), f32)
        tiles = (zero, zero, zero)
        for k in range(n_cl):
            cams = oc_ref[k : k + 1, :]
            lands = ol_ref[k : k + 1, :]
            jac[k, 0] = rows_of([cj_ref[k, 0:9, :]], 16)
            jac[k, 1] = rows_of([cj_ref[k, 9:18, :]], 16)
            one_cam[k] = jnp.where(cam_iota == cams, 1.0, 0.0).astype(jnp.bfloat16).T
            one_land[k] = jnp.where(cam_iota == lands, 1.0, 0.0).astype(jnp.bfloat16).T
            match = jnp.where(keys_t[:, k : k + 1] == keys_f[k : k + 1, :], 1.0, 0.0).astype(
                jnp.bfloat16
            )
            j0, j1 = jac[k, 0], jac[k, 1]
            ka = [lj_ref[k, b : b + 1, :] for b in range(3)]
            kb = [lj_ref[k, 3 + b : 4 + b, :] for b in range(3)]
            e0, e1 = re_ref[k, 0:1, :], re_ref[k, 1:2, :]
            stats = [
                ka[i] * ka[j] + kb[i] * kb[j]
                for i, j in ((0, 0), (0, 1), (0, 2), (1, 1), (1, 2), (2, 2))
            ] + [ka[b] * e0 + kb[b] * e1 for b in range(3)]
            total = exact_dot(rows_of(stats, 16), one_land[k])
            v = [total[i : i + 1] for i in range(9)]
            v[0], v[3], v[5] = v[0] + DAMPING, v[3] + DAMPING, v[5] + DAMPING
            factor = cholesky_three(v[:6])
            base = normal_solve(factor, v[6], v[7], v[8])
            table = rows_of(list(factor) + list(base), 16)
            fac[k] = table
            at_obs = lane_gather(table, lands)
            f = [at_obs[i : i + 1] for i in range(6)]
            g = [at_obs[6 + b : 7 + b] for b in range(3)]
            solved = lower_solve(f, *[j0 * ka[b] + j1 * kb[b] for b in range(3)])
            paired = exact_dot(jnp.concatenate(solved, axis=0), match)
            diag = j0 * j0 + j1 * j1
            for b in range(3):
                diag = diag - solved[b] * paired[16 * b : 16 * b + 16]
            w0 = ka[0] * g[0] + ka[1] * g[1] + ka[2] * g[2] - e0
            w1 = kb[0] * g[0] + kb[1] * g[1] + kb[2] * g[2] - e1
            right = j0 * w0 + j1 * w1
            out = exact_dot(jnp.concatenate([right, diag], axis=0), one_cam[k])
            tiles = place(tiles, out, k)
        for i in range(3):
            msg1[i, 0:9, :] = tiles[i][0:9]
            extra = tiles[i][16:32] + damp if i == 0 else tiles[i][16:32]
            msg1[i, 9:18, :] = extra[0:9]

        pl.semaphore_wait(barrier, n_row + n_col - 2)

        hub_of = ((row, hub_col), (2 * col, col), (2 * col + 1, col))

        def contribution(msg, buf, send, recv, i):
            row_slot = lax.rem(col - hub_col + n_col, n_col)
            slot = (
                row_slot if i == 0 else n_col + lax.rem(row - (2 * col + i - 1) + n_row, n_row)
            )
            return pltpu.make_async_remote_copy(
                src_ref=msg.at[i],
                dst_ref=buf.at[slot],
                send_sem=send.at[i],
                recv_sem=recv.at[slot],
                device_id=hub_of[i],
                device_id_type=MESH,
            )

        def not_self(i):
            return jnp.logical_not(is_hub) if i == 0 else row != 2 * col + (i - 1)

        def to_hubs(msg, buf, send, recv):
            for i in range(3):
                @pl.when(not_self(i))
                def _():
                    contribution(msg, buf, send, recv, i).start()

        def sent_to_hubs(msg, buf, send, recv):
            for i in range(3):
                @pl.when(not_self(i))
                def _():
                    contribution(msg, buf, send, recv, i).wait_send()

        def at_hub(msg, buf, send, recv):
            mine_tile = 1 + row - 2 * col
            total = msg[0] + msg[mine_tile]
            for slot in [*range(1, n_col), *range(n_col + 1, n_col + n_row)]:
                pltpu.make_async_remote_copy(
                    src_ref=msg.at[0],
                    dst_ref=buf.at[slot],
                    send_sem=send.at[0],
                    recv_sem=recv.at[slot],
                    device_id=(row, over(1)),
                    device_id_type=MESH,
                ).wait_recv()
            for slot in [*range(1, n_col), *range(n_col + 1, n_col + n_row)]:
                total = total + buf[slot]
            return total

        def spread_copy(buf, send, recv, j):
            mine_tile = 1 + row - 2 * col
            if j < n_col:
                target, slot = (row, over(j)), 0
            else:
                target, slot = (up(j - n_col), col), mine_tile
            return pltpu.make_async_remote_copy(
                src_ref=buf.at[0],
                dst_ref=buf.at[slot],
                send_sem=send.at[j],
                recv_sem=recv.at[slot],
                device_id=target,
                device_id_type=MESH,
            )

        others = [*range(n_col + 1, n_col + n_row), *range(1, n_col)]

        def spread(buf, send, recv):
            for j in others:
                spread_copy(buf, send, recv, j).start()

        def spread_done(buf, send, recv):
            @pl.when(is_hub)
            def _():
                for j in others:
                    spread_copy(buf, send, recv, j).wait_send()

        def arrived(buf, send, recv):
            for i in range(3):
                @pl.when(not_self(i))
                def _():
                    pltpu.make_async_remote_copy(
                        src_ref=buf.at[0],
                        dst_ref=buf.at[i],
                        send_sem=send.at[1],
                        recv_sem=recv.at[i],
                        device_id=(row, over(1)),
                        device_id_type=MESH,
                    ).wait_recv()

        def tile_of(buf, i):
            return rows_of([buf[i]], 16)

        def pushed(vec, k):
            at_obs = lane_gather(vec, oc_ref[k : k + 1, :])
            m0 = col_sum(jac[k, 0] * at_obs)
            m1 = col_sum(jac[k, 1] * at_obs)
            back = [lj_ref[k, b : b + 1, :] * m0 + lj_ref[k, 3 + b : 4 + b, :] * m1 for b in range(3)]
            total = exact_dot(rows_of(back, 16), one_land[k])
            b = [total[i : i + 1] for i in range(3)]
            factor = [fac[k, i : i + 1, :] for i in range(6)]
            return m0, m1, b, normal_solve(factor, *b)

        to_hubs(msg1, in1, s1, r1)

        @pl.when(is_hub)
        def _():
            total = at_hub(msg1, in1, s1, r1)
            z0 = total[0:9] / total[9:18]
            sums[0] = total[0:9]
            sums[1] = total[9:18]
            zbuf[0] = z0
            zbuf[1 + row - 2 * col] = z0
            spread(zbuf, s2, r2)

        arrived(zbuf, s2, r2)

        z_tiles = tuple(tile_of(zbuf, i) for i in range(3))
        zero = jnp.zeros((16, LANES), f32)
        tiles = (damp * z_tiles[0], zero, zero)
        for k in range(n_cl):
            m0, m1, b, y = pushed(vector_of(z_tiles, k), k)
            yvec[k, 0:3, :] = jnp.concatenate(y, axis=0)
            g = lane_gather(rows_of(list(y), 8), ol_ref[k : k + 1, :])
            w0, w1 = m0, m1
            for i in range(3):
                w0 = w0 - lj_ref[k, i : i + 1, :] * g[i : i + 1]
                w1 = w1 - lj_ref[k, 3 + i : 4 + i, :] * g[i : i + 1]
            out = exact_dot(jac[k, 0] * w0 + jac[k, 1] * w1, one_cam[k])
            tiles = place(tiles, out, k)
        for i in range(3):
            msg2[i] = tiles[i][0:9]
        to_hubs(msg2, in2, s3, r3)
        stot[...] = jnp.zeros_like(stot)

        @pl.when(is_hub)
        def _():
            q0 = at_hub(msg2, in2, s3, r3)
            r0, d = sums[0], sums[1]
            t = q0 / d - zbuf[0]
            tbuf[0] = t
            tbuf[1 + row - 2 * col] = t
            spread(tbuf, s4, r4)
            stot[0:1, :] = col_sum(r0 * zbuf[0])
            stot[1:2, :] = col_sum(r0 * t)
            stot[2:3, :] = col_sum(t * d * t)

        arrived(tbuf, s4, r4)

        t_tiles = tuple(tile_of(tbuf, i) for i in range(3))
        form = col_sum(damp * t_tiles[0] * t_tiles[0])
        for k in range(n_cl):
            m0, m1, b, y = pushed(vector_of(t_tiles, k), k)
            yvec[k, 3:6, :] = jnp.concatenate(y, axis=0)
            square = m0 * m0 + m1 * m1
            for at in range(0, n_obs, LANES):
                form = form + square[:, at : at + LANES]
            form = form - (b[0] * y[0] + b[1] * y[1] + b[2] * y[2])
        stot[3:4, :] = form

        def col_copy(i):
            return pltpu.make_async_remote_copy(
                src_ref=stot,
                dst_ref=sc1.at[i],
                send_sem=s5.at[i],
                recv_sem=r5.at[i],
                device_id=(up(i), col),
                device_id_type=MESH,
            )

        def row_copy(i):
            return pltpu.make_async_remote_copy(
                src_ref=sc2.at[0],
                dst_ref=sc2.at[i],
                send_sem=s6.at[i],
                recv_sem=r6.at[i],
                device_id=(row, over(i)),
                device_id_type=MESH,
            )

        for i in range(1, n_row):
            col_copy(i).start()

        def chosen(tile, first_entry, count):
            entry = lax.broadcasted_iota(jnp.int32, (16, LANES), 1) + first_entry
            level = lax.broadcasted_iota(jnp.int32, (16, LANES), 0)
            entry = jnp.minimum(entry, 143)
            cam = entry // 9
            got = gather_rows(tile, cam + 16 * col)
            return col_sum(jnp.where(entry - 9 * cam == level, got, 0.0))[:, :count]

        z_own = jnp.concatenate([chosen(z_tiles[0], 0, 128), chosen(z_tiles[0], 128, 16)], axis=1)
        t_own = jnp.concatenate([chosen(t_tiles[0], 0, 128), chosen(t_tiles[0], 128, 16)], axis=1)

        total = stot[...]
        for i in range(1, n_row):
            col_copy(i).wait_recv()
        for i in range(1, n_row):
            total = total + sc1[i]
        sc2[0] = total
        for i in range(1, n_col):
            row_copy(i).start()
        for i in range(1, n_col):
            row_copy(i).wait_recv()
        for i in range(1, n_col):
            total = total + sc2[i]
        scalars = jnp.sum(total, axis=1, keepdims=True)
        rz, e, f, h = (scalars[i : i + 1] for i in range(4))
        pq = rz + e
        a0 = rz / pq
        new = a0 * ((rz * f - e * e) / pq)
        g = e / pq + new / rz
        curve = g * g * pq - 2.0 * g * a0 * (e + f) + a0 * a0 * h
        a1 = new / curve
        big_a = a0 + a1 * g
        big_b = -a1 * a0
        cam_ref[...] = big_a * z_own + big_b * t_own
        for k in range(n_cl):
            land_ref[k] = -(fac[k, 6:9, :] + big_a * yvec[k, 0:3, :] + big_b * yvec[k, 3:6, :])

        sent_to_hubs(msg1, in1, s1, r1)
        sent_to_hubs(msg2, in2, s3, r3)
        spread_done(zbuf, s2, r2)
        spread_done(tbuf, s4, r4)
        for i in range(1, n_row):
            col_copy(i).wait_send()
        for i in range(1, n_col):
            row_copy(i).wait_send()

    return kernel


def per_device(cam_jac, land_jac, resid, obs_cam, obs_land, pairs, cam_damp):
    n_row = lax.axis_size("row")
    n_col = lax.axis_size("col")
    n_cl, _, n_obs = cam_jac.shape
    shard = cam_damp.shape[0]
    f32 = jnp.float32
    slots = n_row + n_col
    vmem = pl.BlockSpec(memory_space=pltpu.VMEM)
    dma = pltpu.SemaphoreType.DMA
    cam, land = pl.pallas_call(
        make_kernel(n_row, n_col, n_cl, n_obs),
        out_shape=(
            jax.ShapeDtypeStruct((1, shard), f32),
            jax.ShapeDtypeStruct((n_cl, 3, LANES), f32),
        ),
        in_specs=[pl.BlockSpec(memory_space=pltpu.SMEM)] + [vmem] * 6,
        out_specs=(vmem, vmem),
        scratch_shapes=[
            pltpu.VMEM((n_cl, 2, 16, n_obs), f32),
            pltpu.VMEM((n_cl, n_obs, LANES), jnp.bfloat16),
            pltpu.VMEM((n_cl, n_obs, LANES), jnp.bfloat16),
            pltpu.VMEM((n_cl, 16, LANES), f32),
            pltpu.VMEM((n_cl, 8, LANES), f32),
            pltpu.VMEM((3, 18, LANES), f32),
            pltpu.VMEM((3, 9, LANES), f32),
            pltpu.VMEM((2, 9, LANES), f32),
            pltpu.VMEM((slots, 18, LANES), f32),
            pltpu.VMEM((slots, 9, LANES), f32),
            pltpu.VMEM((3, 9, LANES), f32),
            pltpu.VMEM((3, 9, LANES), f32),
            pltpu.VMEM((n_row, 4, LANES), f32),
            pltpu.VMEM((n_col, 4, LANES), f32),
            pltpu.VMEM((4, LANES), f32),
            dma((3,)), dma((slots,)),
            dma((slots,)), dma((3,)),
            dma((3,)), dma((slots,)),
            dma((slots,)), dma((3,)),
            dma((n_row,)), dma((n_row,)),
            dma((n_col,)), dma((n_col,)),
        ],
        compiler_params=pltpu.CompilerParams(collective_id=0, has_side_effects=True),
        name="schur_step",
    )(pairs, cam_jac, land_jac, resid, obs_cam, obs_land, cam_damp.reshape(1, shard))
    return cam.reshape(shard), land


def solution(mesh):
    in_specs = (
        P(("row", "col"), None, None),
        P(("row", "col"), None, None),
        P(("row", "col"), None, None),
        P(("row", "col"), None),
        P(("row", "col"), None),
        P(("row", "col"), None),
        P(("row", "col")),
    )
    out_specs = (P(("row", "col")), P(("row", "col"), None, None))
    return jax.shard_map(
        per_device, mesh=mesh, in_specs=in_specs, out_specs=out_specs, check_vma=False
    )
```

```python
import jax
import jax.numpy as jnp
from jax import lax
from jax.experimental import pallas as pl
from jax.experimental.pallas import tpu as pltpu
from jax.sharding import PartitionSpec as P

DAMPING = 1.0
MESH = pl.DeviceIdType.MESH
LANES = 128
SIDE = 4
VMEM = 8 << 20


def lane_gather(table, index):
    dims = lax.GatherDimensionNumbers((), (1,), (1,), (0,), (0,))
    pieces = [
        lax.gather(
            table,
            index[at : at + 8, :, None],
            dims,
            slice_sizes=(1, 1),
            mode=lax.GatherScatterMode.PROMISE_IN_BOUNDS,
        )
        for at in range(0, index.shape[0], 8)
    ]
    return pieces[0] if len(pieces) == 1 else jnp.concatenate(pieces, axis=0)


def three_parts(x):
    high = x.astype(jnp.bfloat16).astype(jnp.float32)
    rest = x - high
    mid = rest.astype(jnp.bfloat16).astype(jnp.float32)
    return high, mid, rest - mid


def dot_nt(x, onehot):
    return lax.dot_general(
        x, onehot, (((1,), (1,)), ((), ())), preferred_element_type=jnp.float32
    )


def stacked_parts(x):
    high = x.astype(jnp.bfloat16)
    rest = x - high.astype(jnp.float32)
    mid = rest.astype(jnp.bfloat16)
    low = (rest - mid.astype(jnp.float32)).astype(jnp.bfloat16)
    return jnp.concatenate([high, mid, low], axis=0)


def add_parts(out):
    rows = out.shape[0] // 3
    return out[:rows] + (out[rows : 2 * rows] + out[2 * rows :])


def col_sum(x):
    return jnp.sum(x, axis=0, keepdims=True)


def lower_solve(f, a, b, c):
    one = a * f[0]
    two = (b - f[1] * one) * f[3]
    three = (c - f[2] * one - f[4] * two) * f[5]
    return one, two, three


def upper_solve(f, a, b, c):
    three = c * f[5]
    two = (b - f[4] * three) * f[3]
    one = (a - f[1] * two - f[2] * three) * f[0]
    return one, two, three


def normal_solve(f, a, b, c):
    return upper_solve(f, *lower_solve(f, a, b, c))


def cholesky_three(v):
    inv_first = 1.0 / jnp.sqrt(v[0])
    low_one = v[1] * inv_first
    low_two = v[2] * inv_first
    inv_second = 1.0 / jnp.sqrt(v[3] - low_one * low_one)
    low_three = (v[4] - low_two * low_one) * inv_second
    inv_third = 1.0 / jnp.sqrt(v[5] - low_two * low_two - low_three * low_three)
    return inv_first, low_one, low_two, inv_second, low_three, inv_third


def make_kernel(n_row, n_col, n_cl, n_obs):
    f32 = jnp.float32

    tiles_n = n_obs // LANES
    dense = tiles_n * n_cl

    def kernel(
        pairs_in, cj_in, lj_in, re_in, oc_in, ol_in, damp_in,
        cam_ref, land_ref,
        pairs_ref, cj_ref, lj_ref, re_ref, oc_ref, ol_ref, damp_ref, s0,
        one_cam, one_land, ustat, wstat, xstat, bstat, res, vecs, fac, yvec,
        msg1, msg2, sums, in1, in2, zbuf, tbuf, own, stot,
        s1, r1, s2, r2, s3, r3, s4, r4, s5, r5,
    ):
        one = jnp.asarray(1, jnp.bfloat16)
        nil = jnp.asarray(0, jnp.bfloat16)
        row = lax.axis_index("row")
        col = lax.axis_index("col")
        hub_col = row // 2
        is_hub = col == hub_col
        z, x = row // SIDE, lax.rem(row, SIDE)
        zs = [lax.rem(z + d, SIDE) * SIDE for d in range(SIDE)]
        xs = [lax.rem(x + d, SIDE) for d in range(SIDE)]
        cols = [lax.rem(col + d, n_col) for d in range(n_col)]
        up = lambda i: zs[i // SIDE] + xs[i % SIDE]
        over = lambda i: cols[i]

        def apart(i):
            return sum(min(d, SIDE - d) for d in (i // SIDE, i % SIDE))

        plane = sorted(range(1, n_row), key=lambda i: -apart(i))
        ring = [*range(2, n_col - 1), 1, n_col - 1]

        loads = [
            pltpu.make_async_copy(source, target, s0.at[n])
            for n, (source, target) in enumerate(
                (
                    (oc_in, oc_ref),
                    (ol_in, ol_ref),
                    (lj_in, lj_ref),
                    (re_in, re_ref),
                    (cj_in, cj_ref),
                    (pairs_in, pairs_ref),
                    (damp_in, damp_ref),
                )
            )
        ]
        for load in loads:
            load.start()

        barrier = pltpu.get_barrier_semaphore()

        @pl.when(is_hub)
        def _():
            for i in plane:
                pl.semaphore_signal(barrier, inc=1, device_id=(up(i), col), device_id_type=MESH)
            for i in range(1, n_col):
                pl.semaphore_signal(barrier, inc=1, device_id=(row, over(i)), device_id_type=MESH)

        def place(tiles, out, k):
            rolled = pltpu.roll(out, 64, axis=1)
            half = lax.broadcasted_iota(jnp.int32, out.shape, 1) < 64

            def pick(cond, x):
                return jnp.where(cond, x, 0.0)

            a, b = first[k], second[k]
            return (
                tiles[0] + jnp.where(half, pick(a == 0, out), pick(a == 1, rolled)),
                tiles[1] + jnp.where(half, pick(b == 0, rolled), pick(b == 1, out)),
                tiles[2] + jnp.where(half, pick(b == 2, rolled), pick(b == 3, out)),
            )

        def jac(r, a):
            return cj_ref[(r * 9 + a) * dense : (r * 9 + a + 1) * dense, :]

        def land_jac(r, b):
            return lj_ref[(r * 3 + b) * dense : (r * 3 + b + 1) * dense, :]

        def put(ref, q, value):
            ref[q * dense : (q + 1) * dense, :] = value

        def of_cluster(ref, k, rows):
            return jnp.concatenate(
                [ref[pl.ds(j * n_cl + k, rows, stride=dense), :] for j in range(tiles_n)], axis=1
            )

        def put_result(k, value):
            rows = value.shape[0]
            res[k * 32 : k * 32 + rows, :] = value
            res[(k + n_cl) * 32 : (k + n_cl) * 32 + rows, :] = value

        def result(q):
            return res[pl.ds(q, 2 * n_cl, stride=32), :]

        loads[0].wait()
        loads[1].wait()
        cams = oc_ref[...]
        lands = ol_ref[...]

        cams_f = cams.astype(f32)
        lands_f = lands.astype(f32)

        def packed_row(x, j, k):
            at = j * n_cl + k
            return jnp.broadcast_to(x[at : at + 1, :], (16, LANES)).astype(jnp.bfloat16)

        level = [
            (lax.broadcasted_iota(jnp.int32, (16, LANES), 0) + 16 * i).astype(f32).astype(jnp.bfloat16)
            for i in range(8)
        ]
        for k in range(n_cl):
            for j in range(tiles_n):
                land_row = packed_row(lands_f, j, k)
                cam_row = packed_row(cams_f, j, k)
                for i in range(8):
                    at = (k, slice(16 * i, 16 * i + 16), slice(j * LANES, (j + 1) * LANES))
                    one_land[at] = jnp.where(level[i] == land_row, one, nil)
                    one_cam[at] = jnp.where(level[i] == cam_row, one, nil)

        power = jnp.full((dense, LANES), 2.0**-64, f32)
        for i in range(7):
            power = power * jnp.where(((cams >> i) & 1) == 1, 2.0 ** (2**i), 1.0)
        code = power * (1.0 + lands_f * (1.0 / 128.0))
        code_t = code.T

        zero = jnp.zeros((dense, LANES), f32)
        for q in range(27, 32):
            put(xstat, q, zero)
            put(ustat, q, zero)
        for q in range(18, 24):
            put(wstat, q, zero)
        for q in range(9, 16):
            put(bstat, q, zero)
        loads[2].wait()
        loads[3].wait()
        ka = [land_jac(0, b) for b in range(3)]
        kb = [land_jac(1, b) for b in range(3)]
        e0, e1 = (
            jnp.concatenate(
                [re_ref[pl.ds(2 * j + r, n_cl, stride=2 * tiles_n), :] for j in range(tiles_n)], axis=0
            )
            for r in range(2)
        )
        stats = [
            ka[i] * ka[j] + kb[i] * kb[j]
            for i, j in ((0, 0), (0, 1), (0, 2), (1, 1), (1, 2), (2, 2))
        ] + [ka[b] * e0 + kb[b] * e1 for b in range(3)]
        for q, stat in enumerate(stats):
            for p, part in enumerate(three_parts(stat)):
                put(xstat, p * 9 + q, part)
        for k in range(n_cl):
            put_result(k, dot_nt(of_cluster(xstat, k, 32).astype(jnp.bfloat16), one_land[k]))
        v = [result(q) + (result(9 + q) + result(18 + q)) for q in range(9)]
        v[0], v[3], v[5] = v[0] + DAMPING, v[3] + DAMPING, v[5] + DAMPING
        factor = cholesky_three(v[:6])
        base = normal_solve(factor, v[6], v[7], v[8])
        for i in range(6):
            fac[i] = factor[i]
        for b in range(3):
            yvec[b] = base[b]

        loads[4].wait()
        loads[5].wait()
        loads[6].wait()
        first = [pairs_ref[0, k] - 2 * row for k in range(n_cl)]
        second = [pairs_ref[1, k] - 4 * col for k in range(n_cl)]

        lane = lax.broadcasted_iota(jnp.int32, (16, LANES), 1)
        sub = lax.broadcasted_iota(jnp.int32, (16, LANES), 0)
        flat = (lane - 16 * col) * 9 + sub
        mine = (lane >= 16 * col) & (lane < 16 * col + 16) & (sub < 9)
        flat = jnp.where(mine, flat, 0)
        damp_low = jnp.broadcast_to(damp_ref[:, :LANES], (8, LANES))
        damp_high = jnp.broadcast_to(
            jnp.concatenate([damp_ref[:, LANES:], jnp.zeros((1, 2 * LANES - 144), f32)], axis=1),
            (8, LANES),
        )
        damp = jnp.where(
            flat < LANES,
            lane_gather(damp_low, jnp.minimum(flat, LANES - 1)),
            lane_gather(damp_high, jnp.maximum(flat - LANES, 0)),
        )
        damp = jnp.where(mine, damp, 0.0)

        f = [lane_gather(factor[i], lands) for i in range(6)]
        g = [lane_gather(base[b], lands) for b in range(3)]
        w0 = ka[0] * g[0] + ka[1] * g[1] + ka[2] * g[2] - e0
        w1 = kb[0] * g[0] + kb[1] * g[1] + kb[2] * g[2] - e1
        for a in range(9):
            j0, j1 = jac(0, a), jac(1, a)
            solved = lower_solve(f, *[j0 * ka[b] + j1 * kb[b] for b in range(3)])
            for b in range(3):
                put(ustat, b * 8 + a if a < 8 else 24 + b, solved[b])
            put(wstat, a if a < 8 else 16, j0 * w0 + j1 * w1)
            put(wstat, 8 + a if a < 8 else 17, j0 * j0 + j1 * j1)
        zero = jnp.zeros((32, LANES), f32)
        tiles = (zero, zero, zero)
        for k in range(n_cl):
            rows_packed = [
                jnp.concatenate([packed_row(code, j, k)] * 8, axis=0) for j in range(tiles_n)
            ]
            blocks = []
            for j in range(tiles_n):
                at = j * n_cl + k
                column = jnp.broadcast_to(code_t[:, at : at + 1], (LANES, LANES)).astype(jnp.bfloat16)
                blocks.append(
                    jnp.concatenate([jnp.where(column == r, one, nil) for r in rows_packed], axis=1)
                )
            match = jnp.concatenate(blocks, axis=0)
            solved = of_cluster(ustat, k, 32)
            paired = add_parts(
                jnp.dot(stacked_parts(solved), match, preferred_element_type=jnp.float32)
            )
            square = solved * paired
            plain = of_cluster(wstat, k, 24)
            diag = plain[8:16] - (square[0:8] + square[8:16] + square[16:24])
            lhs = jnp.concatenate([plain[0:8], diag, plain[16:24], square[24:32]], axis=0)
            tiles = place(tiles, add_parts(dot_nt(stacked_parts(lhs), one_cam[k])), k)
        for i in range(3):
            extra = damp if i == 0 else jnp.zeros((16, LANES), f32)
            t = tiles[i]
            msg1[i, 0:8, :] = t[0:8]
            msg1[i, 8:16, :] = t[8:16] + extra[0:8]
            msg1[i, 16:17, :] = t[16:17]
            msg1[i, 17:18, :] = t[17:18] - (t[24:25] + t[25:26] + t[26:27]) + extra[8:9]

        pl.semaphore_wait(barrier, jnp.where(is_hub, 1, 3))

        hub_of = ((row, hub_col), (2 * col, col), (2 * col + 1, col))

        def contribution(msg, buf, send, recv, i):
            row_slot = lax.rem(col - hub_col + n_col, n_col)
            hub_z, hub_x = (2 * col + i - 1) // SIDE, lax.rem(2 * col + i - 1, SIDE)
            plane_slot = lax.rem(z - hub_z + SIDE, SIDE) * SIDE + lax.rem(x - hub_x + SIDE, SIDE)
            slot = row_slot if i == 0 else n_col + plane_slot
            return pltpu.make_async_remote_copy(
                src_ref=msg.at[i],
                dst_ref=buf.at[slot],
                send_sem=send.at[i],
                recv_sem=recv.at[slot],
                device_id=hub_of[i],
                device_id_type=MESH,
            )

        def not_self(i):
            return jnp.logical_not(is_hub) if i == 0 else row != 2 * col + (i - 1)

        def to_hubs(msg, buf, send, recv):
            for i in range(3):
                @pl.when(not_self(i))
                def _():
                    contribution(msg, buf, send, recv, i).start()

        def sent_to_hubs(msg, buf, send, recv):
            for i in range(3):
                @pl.when(not_self(i))
                def _():
                    contribution(msg, buf, send, recv, i).wait_send()

        def at_hub(msg, buf, send, recv):
            mine_tile = 1 + row - 2 * col
            total = msg[0] + msg[mine_tile]
            late = [n_col + i for i in plane[::-1]]
            for slot in [*ring, *late]:
                pltpu.make_async_remote_copy(
                    src_ref=msg.at[0],
                    dst_ref=buf.at[slot],
                    send_sem=send.at[0],
                    recv_sem=recv.at[slot],
                    device_id=(row, over(1)),
                    device_id_type=MESH,
                ).wait_recv()
            for slot in [*ring, *late]:
                total = total + buf[slot]
            return total

        def spread_copy(buf, send, recv, j):
            mine_tile = 1 + row - 2 * col
            if j < n_col:
                target, slot = (row, over(j)), 0
            else:
                target, slot = (up(j - n_col), col), mine_tile
            return pltpu.make_async_remote_copy(
                src_ref=buf.at[0],
                dst_ref=buf.at[slot],
                send_sem=send.at[j],
                recv_sem=recv.at[slot],
                device_id=target,
                device_id_type=MESH,
            )

        others = [*[n_col + i for i in plane], *ring]

        def spread(buf, send, recv):
            for j in others:
                spread_copy(buf, send, recv, j).start()

        def spread_done(buf, send, recv):
            @pl.when(is_hub)
            def _():
                for j in others:
                    spread_copy(buf, send, recv, j).wait_send()

        def arrived(buf, send, recv):
            for i in range(3):
                @pl.when(not_self(i))
                def _():
                    pltpu.make_async_remote_copy(
                        src_ref=buf.at[0],
                        dst_ref=buf.at[i],
                        send_sem=send.at[1],
                        recv_sem=recv.at[i],
                        device_id=(row, over(1)),
                        device_id_type=MESH,
                    ).wait_recv()

        left = lax.broadcasted_iota(jnp.int32, (9, LANES), 1) < 64

        def pushed(tiles):
            rolled = [pltpu.roll(t, 64, axis=1) for t in tiles]
            for k in range(n_cl):
                a, b = first[k], second[k]
                own = jnp.where(a == 0, tiles[0], rolled[0])
                odd = jnp.where(b < 2, tiles[1], tiles[2])
                even = jnp.where(b < 2, rolled[1], rolled[2])
                vec = jnp.where(left, own, jnp.where((b == 1) | (b == 3), odd, even))
                vecs[k * 16 : k * 16 + 9, :] = vec
                vecs[(k + n_cl) * 16 : (k + n_cl) * 16 + 9, :] = vec
            m0 = m1 = None
            for a in range(9):
                at_obs = lane_gather(vecs[pl.ds(a, 2 * n_cl, stride=16), :], cams)
                p0, p1 = jac(0, a) * at_obs, jac(1, a) * at_obs
                m0, m1 = (p0, p1) if m0 is None else (m0 + p0, m1 + p1)
            for b in range(3):
                back = land_jac(0, b) * m0 + land_jac(1, b) * m1
                for p, part in enumerate(three_parts(back)):
                    put(bstat, p * 3 + b, part)
            for k in range(n_cl):
                put_result(k, dot_nt(of_cluster(bstat, k, 16).astype(jnp.bfloat16), one_land[k]))
            total = [result(b) + (result(3 + b) + result(6 + b)) for b in range(3)]
            return m0, m1, total, normal_solve([fac[i] for i in range(6)], *total)

        to_hubs(msg1, in1, s1, r1)

        @pl.when(is_hub)
        def _():
            total = at_hub(msg1, in1, s1, r1)
            sums[...] = total
            zbuf[0, 0:8, :] = total[0:8] / total[8:16]
            zbuf[0, 8:9, :] = total[16:17] / total[17:18]
            spread(zbuf, s2, r2)
            zbuf[1 + row - 2 * col] = zbuf[0]

        arrived(zbuf, s2, r2)

        z_tiles = tuple(zbuf[i] for i in range(3))
        m0, m1, b, y = pushed(z_tiles)
        for i in range(3):
            yvec[3 + i] = y[i]
        w0, w1 = m0, m1
        for i in range(3):
            g = lane_gather(y[i], lands)
            w0 = w0 - land_jac(0, i) * g
            w1 = w1 - land_jac(1, i) * g
        for a in range(9):
            for p, part in enumerate(three_parts(jac(0, a) * w0 + jac(1, a) * w1)):
                put(xstat, p * 8 + a if a < 8 else 24 + p, part)
        zero = jnp.zeros((16, LANES), f32)
        tiles = (zero, zero, zero)
        for k in range(n_cl):
            out = dot_nt(of_cluster(xstat, k, 32).astype(jnp.bfloat16), one_cam[k])
            out = jnp.concatenate([out[0:8] + (out[8:16] + out[16:24]), out[24:32]], axis=0)
            tiles = place(tiles, out, k)
        for i in range(3):
            t = tiles[i]
            low, high = t[0:8], t[8:9] + (t[9:10] + t[10:11])
            if i == 0:
                low = low + damp[0:8] * z_tiles[0][0:8]
                high = high + damp[8:9] * z_tiles[0][8:9]
            msg2[i, 0:8, :] = low
            msg2[i, 8:9, :] = high
        to_hubs(msg2, in2, s3, r3)
        own[...] = jnp.zeros_like(own)

        @pl.when(is_hub)
        def _():
            q0 = at_hub(msg2, in2, s3, r3)
            total = sums[...]
            d_low, d_high = total[8:16], total[17:18]
            z_low, z_high = zbuf[0, 0:8, :], zbuf[0, 8:9, :]
            t_low = q0[0:8] / d_low - z_low
            t_high = q0[8:9] / d_high - z_high
            tbuf[0, 0:8, :] = t_low
            tbuf[0, 8:9, :] = t_high
            spread(tbuf, s4, r4)
            tbuf[1 + row - 2 * col] = tbuf[0]
            r_low, r_high = total[0:8], total[16:17]
            own[0:1, :] = col_sum(r_low * z_low) + r_high * z_high
            own[1:2, :] = col_sum(r_low * t_low) + r_high * t_high
            own[2:3, :] = col_sum(t_low * d_low * t_low) + t_high * d_high * t_high

        arrived(tbuf, s4, r4)

        t_tiles = tuple(tbuf[i] for i in range(3))
        m0, m1, b, y = pushed(t_tiles)
        for i in range(3):
            yvec[6 + i] = y[i]
        square = m0 * m0 + m1 * m1
        form = -0.5 * (b[0] * y[0] + b[1] * y[1] + b[2] * y[2])
        for at in range(0, dense, 8):
            form = form + square[at : at + 8]
        t = t_tiles[0]
        form = form + damp[0:8] * t[0:8] * t[0:8]
        own[3:4, :] = col_sum(form) + damp[8:9] * t[8:9] * t[8:9]

        quarter = lax.broadcasted_iota(jnp.int32, (4, LANES), 1) // 32
        which = lax.broadcasted_iota(jnp.int32, (4, LANES), 0)
        four = own[...]
        four = four + pltpu.roll(four, 64, axis=1)
        four = four + pltpu.roll(four, 32, axis=1)
        stot[0:1, :] = col_sum(jnp.where(quarter == which, four, 0.0))

        def total_copy(i, j):
            slot = i * n_col + j
            return pltpu.make_async_remote_copy(
                src_ref=stot.at[pl.ds(0, 1)],
                dst_ref=stot.at[pl.ds(slot, 1)],
                send_sem=s5,
                recv_sem=r5,
                device_id=(up(i), over(j)),
                device_id_type=MESH,
            )

        def total_wait():
            return pltpu.make_async_remote_copy(
                src_ref=stot.at[pl.ds(1, n_row * n_col - 1)],
                dst_ref=stot.at[pl.ds(1, n_row * n_col - 1)],
                send_sem=s5,
                recv_sem=r5,
                device_id=(row, over(1)),
                device_id_type=MESH,
            )

        far = sorted(
            [(i, j) for i in range(n_row) for j in range(n_col) if i or j],
            key=lambda ij: -(apart(ij[0]) + min(ij[1], n_col - ij[1]) / 2),
        )
        for i, j in far:
            total_copy(i, j).start()

        def chosen(tile, first_entry, count):
            entry = lax.broadcasted_iota(jnp.int32, (8, LANES), 1) + first_entry
            level = lax.broadcasted_iota(jnp.int32, (8, LANES), 0)
            entry = jnp.minimum(entry, 143)
            cam = entry // 9
            rest = entry - 9 * cam
            at = cam + 16 * col
            low = jnp.where(rest == level, lane_gather(tile[0:8], at), 0.0)
            high = lane_gather(jnp.broadcast_to(tile[8:9], (8, LANES)), at)
            return col_sum(low + jnp.where((rest == 8) & (level == 0), high, 0.0))[:, :count]

        z_own = jnp.concatenate([chosen(z_tiles[0], 0, 128), chosen(z_tiles[0], 128, 16)], axis=1)
        t_own = jnp.concatenate([chosen(t_tiles[0], 0, 128), chosen(t_tiles[0], 128, 16)], axis=1)

        sent_to_hubs(msg1, in1, s1, r1)
        sent_to_hubs(msg2, in2, s3, r3)
        spread_done(zbuf, s2, r2)
        spread_done(tbuf, s4, r4)
        total_wait().wait_recv()
        total = jnp.where(quarter == which, col_sum(stot[...]), 0.0)
        scalars = jnp.sum(total, axis=1, keepdims=True)
        rz, e, f, h = (scalars[i : i + 1] for i in range(4))
        pq = rz + e
        a0 = rz / pq
        new = a0 * ((rz * f - e * e) / pq)
        g = e / pq + new / rz
        curve = g * g * pq - 2.0 * g * a0 * (e + f) + a0 * a0 * h
        a1 = new / curve
        big_a = a0 + a1 * g
        big_b = -a1 * a0
        cam_ref[...] = big_a * z_own + big_b * t_own
        for b in range(3):
            land = -(yvec[b] + big_a * yvec[3 + b] + big_b * yvec[6 + b])
            land_ref[b] = land[0:n_cl]
        total_wait().wait_send()

    return kernel


def per_device(cam_jac, land_jac, resid, obs_cam, obs_land, pairs, cam_damp):
    n_row = lax.axis_size("row")
    n_col = lax.axis_size("col")
    n_cl, _, n_obs = cam_jac.shape
    shard = cam_damp.shape[0]
    f32 = jnp.float32
    slots = n_row + n_col
    tiles = n_obs // LANES
    dense = n_cl * tiles
    vmem = pl.BlockSpec(memory_space=pltpu.VMEM)
    dma = pltpu.SemaphoreType.DMA

    def entries_first(x):
        return (
            x.reshape(n_cl, -1, tiles, LANES).transpose(1, 2, 0, 3).reshape(-1, LANES)
        )

    cam, land = pl.pallas_call(
        make_kernel(n_row, n_col, n_cl, n_obs),
        out_shape=(
            jax.ShapeDtypeStruct((1, shard), f32),
            jax.ShapeDtypeStruct((3, n_cl, LANES), f32),
        ),
        in_specs=[pl.BlockSpec(memory_space=pltpu.HBM)] * 7,
        out_specs=(vmem, vmem),
        scratch_shapes=[
            pltpu.SMEM((2, n_cl), jnp.int32),
            pltpu.VMEM((18 * dense, LANES), f32),
            pltpu.VMEM((6 * dense, LANES), f32),
            pltpu.VMEM((2 * dense, LANES), f32),
            pltpu.VMEM((dense, LANES), jnp.int32),
            pltpu.VMEM((dense, LANES), jnp.int32),
            pltpu.VMEM((1, shard), f32),
            dma((7,)),
            pltpu.VMEM((n_cl, LANES, n_obs), jnp.bfloat16),
            pltpu.VMEM((n_cl, LANES, n_obs), jnp.bfloat16),
            pltpu.VMEM((32 * dense, LANES), f32),
            pltpu.VMEM((24 * dense, LANES), f32),
            pltpu.VMEM((32 * dense, LANES), f32),
            pltpu.VMEM((16 * dense, LANES), f32),
            pltpu.VMEM((2 * n_cl * 32, LANES), f32),
            pltpu.VMEM((2 * n_cl * 16, LANES), f32),
            pltpu.VMEM((6, 8, LANES), f32),
            pltpu.VMEM((9, 8, LANES), f32),
            pltpu.VMEM((3, 18, LANES), f32),
            pltpu.VMEM((3, 9, LANES), f32),
            pltpu.VMEM((18, LANES), f32),
            pltpu.VMEM((slots, 18, LANES), f32),
            pltpu.VMEM((slots, 9, LANES), f32),
            pltpu.VMEM((3, 9, LANES), f32),
            pltpu.VMEM((3, 9, LANES), f32),
            pltpu.VMEM((4, LANES), f32),
            pltpu.VMEM((n_row * n_col, LANES), f32),
            dma((3,)), dma((slots,)),
            dma((slots,)), dma((3,)),
            dma((3,)), dma((slots,)),
            dma((slots,)), dma((3,)),
            dma, dma,
        ],
        compiler_params=pltpu.CompilerParams(collective_id=0, has_side_effects=True, vmem_limit_bytes=VMEM),
        name="schur_step",
    )(
        *(
            pltpu.with_memory_space_constraint(x, pltpu.HBM)
            for x in (
        pairs.T,
        entries_first(cam_jac),
        entries_first(land_jac),
        resid.reshape(n_cl, 2, tiles, LANES).transpose(0, 2, 1, 3).reshape(-1, LANES),
        obs_cam.reshape(n_cl, tiles, LANES).transpose(1, 0, 2).reshape(-1, LANES),
        obs_land.reshape(n_cl, tiles, LANES).transpose(1, 0, 2).reshape(-1, LANES),
        cam_damp.reshape(1, shard),
            )
        )
    )
    return cam.reshape(shard), land.transpose(1, 0, 2)


def solution(mesh):
    in_specs = (
        P(("row", "col"), None, None),
        P(("row", "col"), None, None),
        P(("row", "col"), None, None),
        P(("row", "col"), None),
        P(("row", "col"), None),
        P(("row", "col"), None),
        P(("row", "col")),
    )
    out_specs = (P(("row", "col")), P(("row", "col"), None, None))
    return jax.shard_map(
        per_device, mesh=mesh, in_specs=in_specs, out_specs=out_specs, check_vma=False
    )
```

```python
import jax
import jax.numpy as jnp
from jax import lax
from jax.experimental import pallas as pl
from jax.experimental.pallas import tpu as pltpu
from jax.sharding import PartitionSpec as P

DAMPING = 1.0
MESH = pl.DeviceIdType.MESH
LANES = 128
SIDE = 4
VMEM = 8 << 20


def lane_gather(table, index):
    dims = lax.GatherDimensionNumbers((), (1,), (1,), (0,), (0,))
    pieces = [
        lax.gather(
            table,
            index[at : at + 8, :, None],
            dims,
            slice_sizes=(1, 1),
            mode=lax.GatherScatterMode.PROMISE_IN_BOUNDS,
        )
        for at in range(0, index.shape[0], 8)
    ]
    return pieces[0] if len(pieces) == 1 else jnp.concatenate(pieces, axis=0)


def three_parts(x):
    high = x.astype(jnp.bfloat16).astype(jnp.float32)
    rest = x - high
    mid = rest.astype(jnp.bfloat16).astype(jnp.float32)
    return high, mid, rest - mid


def dot_nt(x, onehot):
    return lax.dot_general(
        x, onehot, (((1,), (1,)), ((), ())), preferred_element_type=jnp.float32
    )


def stacked_parts(x):
    high = x.astype(jnp.bfloat16)
    rest = x - high.astype(jnp.float32)
    mid = rest.astype(jnp.bfloat16)
    low = (rest - mid.astype(jnp.float32)).astype(jnp.bfloat16)
    return jnp.concatenate([high, mid, low], axis=0)


def add_parts(out):
    rows = out.shape[0] // 3
    return out[:rows] + (out[rows : 2 * rows] + out[2 * rows :])


def col_sum(x):
    return jnp.sum(x, axis=0, keepdims=True)


def lower_solve(f, a, b, c):
    one = a * f[0]
    two = (b - f[1] * one) * f[3]
    three = (c - f[2] * one - f[4] * two) * f[5]
    return one, two, three


def upper_solve(f, a, b, c):
    three = c * f[5]
    two = (b - f[4] * three) * f[3]
    one = (a - f[1] * two - f[2] * three) * f[0]
    return one, two, three


def normal_solve(f, a, b, c):
    return upper_solve(f, *lower_solve(f, a, b, c))


def cholesky_three(v):
    inv_first = 1.0 / jnp.sqrt(v[0])
    low_one = v[1] * inv_first
    low_two = v[2] * inv_first
    inv_second = 1.0 / jnp.sqrt(v[3] - low_one * low_one)
    low_three = (v[4] - low_two * low_one) * inv_second
    inv_third = 1.0 / jnp.sqrt(v[5] - low_two * low_two - low_three * low_three)
    return inv_first, low_one, low_two, inv_second, low_three, inv_third


def make_kernel(n_row, n_col, n_cl, n_obs):
    f32 = jnp.float32

    tiles_n = n_obs // LANES
    dense = tiles_n * n_cl

    def kernel(
        pairs_in, cj_in, lj_in, re_in, oc_in, ol_in, damp_in,
        cam_ref, land_ref,
        pairs_ref, cj_ref, lj_ref, re_ref, oc_ref, ol_ref, damp_ref, s0,
        one_cam, one_land, ustat, wstat, xstat, bstat, res, vecs, fac, yvec,
        msg1, msg2, in1, zbuf, in2, in3, hsum, qbuf, own, stot,
        s1, r1, s2, r2, s3, r3, s4, r4, s5, r5, s6, r6,
    ):
        one = jnp.asarray(1, jnp.bfloat16)
        nil = jnp.asarray(0, jnp.bfloat16)
        row = lax.axis_index("row")
        col = lax.axis_index("col")
        hub_col = row // 2
        is_hub = col == hub_col
        z, x = row // SIDE, lax.rem(row, SIDE)
        zs = [lax.rem(z + d, SIDE) * SIDE for d in range(SIDE)]
        xs = [lax.rem(x + d, SIDE) for d in range(SIDE)]
        cols = [lax.rem(col + d, n_col) for d in range(n_col)]
        up = lambda i: zs[i // SIDE] + xs[i % SIDE]
        over = lambda i: cols[i]

        def apart(i):
            return sum(min(d, SIDE - d) for d in (i // SIDE, i % SIDE))

        plane = sorted(range(1, n_row), key=lambda i: -apart(i))
        ring = [*range(2, n_col - 1), 1, n_col - 1]

        loads = [
            pltpu.make_async_copy(source, target, s0.at[n])
            for n, (source, target) in enumerate(
                (
                    (oc_in, oc_ref),
                    (ol_in, ol_ref),
                    (lj_in, lj_ref),
                    (re_in, re_ref),
                    (cj_in, cj_ref),
                    (pairs_in, pairs_ref),
                    (damp_in, damp_ref),
                )
            )
        ]
        for load in loads:
            load.start()

        barrier = pltpu.get_barrier_semaphore()

        @pl.when(is_hub)
        def _():
            for i in plane:
                pl.semaphore_signal(barrier, inc=1, device_id=(up(i), col), device_id_type=MESH)
            for i in range(1, n_col):
                pl.semaphore_signal(barrier, inc=1, device_id=(row, over(i)), device_id_type=MESH)

        def place(tiles, out, k):
            rolled = pltpu.roll(out, 64, axis=1)
            half = lax.broadcasted_iota(jnp.int32, out.shape, 1) < 64

            def pick(cond, x):
                return jnp.where(cond, x, 0.0)

            a, b = first[k], second[k]
            return (
                tiles[0] + jnp.where(half, pick(a == 0, out), pick(a == 1, rolled)),
                tiles[1] + jnp.where(half, pick(b == 0, rolled), pick(b == 1, out)),
                tiles[2] + jnp.where(half, pick(b == 2, rolled), pick(b == 3, out)),
            )

        def jac(r, a):
            return cj_ref[(r * 9 + a) * dense : (r * 9 + a + 1) * dense, :]

        def land_jac(r, b):
            return lj_ref[(r * 3 + b) * dense : (r * 3 + b + 1) * dense, :]

        def put(ref, q, value):
            ref[q * dense : (q + 1) * dense, :] = value

        def of_cluster(ref, k, rows):
            return jnp.concatenate(
                [ref[pl.ds(j * n_cl + k, rows, stride=dense), :] for j in range(tiles_n)], axis=1
            )

        def put_result(k, value):
            rows = value.shape[0]
            res[k * 32 : k * 32 + rows, :] = value
            res[(k + n_cl) * 32 : (k + n_cl) * 32 + rows, :] = value

        def result(q):
            return res[pl.ds(q, 2 * n_cl, stride=32), :]

        loads[0].wait()
        loads[1].wait()
        cams = oc_ref[...]
        lands = ol_ref[...]

        cams_f = cams.astype(f32)
        lands_f = lands.astype(f32)

        def packed_row(x, j, k):
            at = j * n_cl + k
            return jnp.broadcast_to(x[at : at + 1, :], (16, LANES)).astype(jnp.bfloat16)

        level = [
            (lax.broadcasted_iota(jnp.int32, (16, LANES), 0) + 16 * i).astype(f32).astype(jnp.bfloat16)
            for i in range(8)
        ]
        for k in range(n_cl):
            for j in range(tiles_n):
                land_row = packed_row(lands_f, j, k)
                cam_row = packed_row(cams_f, j, k)
                for i in range(8):
                    at = (k, slice(16 * i, 16 * i + 16), slice(j * LANES, (j + 1) * LANES))
                    one_land[at] = jnp.where(level[i] == land_row, one, nil)
                    one_cam[at] = jnp.where(level[i] == cam_row, one, nil)

        power = jnp.full((dense, LANES), 2.0**-64, f32)
        for i in range(7):
            power = power * jnp.where(((cams >> i) & 1) == 1, 2.0 ** (2**i), 1.0)
        code = power * (1.0 + lands_f * (1.0 / 128.0))
        code_t = code.T

        zero = jnp.zeros((dense, LANES), f32)
        for q in range(27, 32):
            put(xstat, q, zero)
            put(ustat, q, zero)
        for q in range(18, 24):
            put(wstat, q, zero)
        for q in range(9, 16):
            put(bstat, q, zero)
        loads[2].wait()
        loads[3].wait()
        ka = [land_jac(0, b) for b in range(3)]
        kb = [land_jac(1, b) for b in range(3)]
        e0, e1 = (
            jnp.concatenate(
                [re_ref[pl.ds(2 * j + r, n_cl, stride=2 * tiles_n), :] for j in range(tiles_n)], axis=0
            )
            for r in range(2)
        )
        stats = [
            ka[i] * ka[j] + kb[i] * kb[j]
            for i, j in ((0, 0), (0, 1), (0, 2), (1, 1), (1, 2), (2, 2))
        ] + [ka[b] * e0 + kb[b] * e1 for b in range(3)]
        for q, stat in enumerate(stats):
            for p, part in enumerate(three_parts(stat)):
                put(xstat, p * 9 + q, part)
        for k in range(n_cl):
            put_result(k, dot_nt(of_cluster(xstat, k, 32).astype(jnp.bfloat16), one_land[k]))
        v = [result(q) + (result(9 + q) + result(18 + q)) for q in range(9)]
        v[0], v[3], v[5] = v[0] + DAMPING, v[3] + DAMPING, v[5] + DAMPING
        factor = cholesky_three(v[:6])
        base = normal_solve(factor, v[6], v[7], v[8])
        for i in range(6):
            fac[i] = factor[i]
        for b in range(3):
            yvec[b] = base[b]

        loads[4].wait()
        loads[5].wait()
        loads[6].wait()
        first = [pairs_ref[0, k] - 2 * row for k in range(n_cl)]
        second = [pairs_ref[1, k] - 4 * col for k in range(n_cl)]

        lane = lax.broadcasted_iota(jnp.int32, (16, LANES), 1)
        sub = lax.broadcasted_iota(jnp.int32, (16, LANES), 0)
        flat = (lane - 16 * col) * 9 + sub
        mine = (lane >= 16 * col) & (lane < 16 * col + 16) & (sub < 9)
        flat = jnp.where(mine, flat, 0)
        damp_low = jnp.broadcast_to(damp_ref[:, :LANES], (8, LANES))
        damp_high = jnp.broadcast_to(
            jnp.concatenate([damp_ref[:, LANES:], jnp.zeros((1, 2 * LANES - 144), f32)], axis=1),
            (8, LANES),
        )
        damp = jnp.where(
            flat < LANES,
            lane_gather(damp_low, jnp.minimum(flat, LANES - 1)),
            lane_gather(damp_high, jnp.maximum(flat - LANES, 0)),
        )
        damp = jnp.where(mine, damp, 0.0)

        f = [lane_gather(factor[i], lands) for i in range(6)]
        g = [lane_gather(base[b], lands) for b in range(3)]
        w0 = ka[0] * g[0] + ka[1] * g[1] + ka[2] * g[2] - e0
        w1 = kb[0] * g[0] + kb[1] * g[1] + kb[2] * g[2] - e1
        for a in range(9):
            j0, j1 = jac(0, a), jac(1, a)
            solved = lower_solve(f, *[j0 * ka[b] + j1 * kb[b] for b in range(3)])
            for b in range(3):
                put(ustat, b * 8 + a if a < 8 else 24 + b, solved[b])
            put(wstat, a if a < 8 else 16, j0 * w0 + j1 * w1)
            put(wstat, 8 + a if a < 8 else 17, j0 * j0 + j1 * j1)
        zero = jnp.zeros((32, LANES), f32)
        tiles = (zero, zero, zero)
        for k in range(n_cl):
            rows_packed = [
                jnp.concatenate([packed_row(code, j, k)] * 8, axis=0) for j in range(tiles_n)
            ]
            blocks = []
            for j in range(tiles_n):
                at = j * n_cl + k
                column = jnp.broadcast_to(code_t[:, at : at + 1], (LANES, LANES)).astype(jnp.bfloat16)
                blocks.append(
                    jnp.concatenate([jnp.where(column == r, one, nil) for r in rows_packed], axis=1)
                )
            match = jnp.concatenate(blocks, axis=0)
            solved = of_cluster(ustat, k, 32)
            paired = add_parts(
                jnp.dot(stacked_parts(solved), match, preferred_element_type=jnp.float32)
            )
            square = solved * paired
            plain = of_cluster(wstat, k, 24)
            diag = plain[8:16] - (square[0:8] + square[8:16] + square[16:24])
            lhs = jnp.concatenate([plain[0:8], diag, plain[16:24], square[24:32]], axis=0)
            tiles = place(tiles, add_parts(dot_nt(stacked_parts(lhs), one_cam[k])), k)
        for i in range(3):
            extra = damp if i == 0 else jnp.zeros((16, LANES), f32)
            t = tiles[i]
            msg1[i, 0:8, :] = t[0:8]
            msg1[i, 8:16, :] = t[8:16] + extra[0:8]
            msg1[i, 16:17, :] = t[16:17]
            msg1[i, 17:18, :] = t[17:18] - (t[24:25] + t[25:26] + t[26:27]) + extra[8:9]

        pl.semaphore_wait(barrier, jnp.where(is_hub, 1, 3))

        hub_of = ((row, hub_col), (2 * col, col), (2 * col + 1, col))

        def contribution(msg, buf, send, recv, i):
            row_slot = lax.rem(col - hub_col + n_col, n_col)
            hub_z, hub_x = (2 * col + i - 1) // SIDE, lax.rem(2 * col + i - 1, SIDE)
            plane_slot = lax.rem(z - hub_z + SIDE, SIDE) * SIDE + lax.rem(x - hub_x + SIDE, SIDE)
            slot = row_slot if i == 0 else n_col + plane_slot
            return pltpu.make_async_remote_copy(
                src_ref=msg.at[i],
                dst_ref=buf.at[slot],
                send_sem=send.at[i],
                recv_sem=recv.at[slot],
                device_id=hub_of[i],
                device_id_type=MESH,
            )

        def not_self(i):
            return jnp.logical_not(is_hub) if i == 0 else row != 2 * col + (i - 1)

        def to_hubs(msg, buf, send, recv):
            for i in range(3):
                @pl.when(not_self(i))
                def _():
                    contribution(msg, buf, send, recv, i).start()

        def sent_to_hubs(msg, buf, send, recv):
            for i in range(3):
                @pl.when(not_self(i))
                def _():
                    contribution(msg, buf, send, recv, i).wait_send()

        def at_hub(msg, buf, send, recv):
            mine_tile = 1 + row - 2 * col
            total = msg[0] + msg[mine_tile]
            late = [n_col + i for i in plane[::-1]]
            for slot in [*ring, *late]:
                pltpu.make_async_remote_copy(
                    src_ref=msg.at[0],
                    dst_ref=buf.at[slot],
                    send_sem=send.at[0],
                    recv_sem=recv.at[slot],
                    device_id=(row, over(1)),
                    device_id_type=MESH,
                ).wait_recv()
            for slot in [*ring, *late]:
                total = total + buf[slot]
            return total

        def spread_copy(buf, send, recv, j):
            mine_tile = 1 + row - 2 * col
            if j < n_col:
                target, slot = (row, over(j)), 0
            else:
                target, slot = (up(j - n_col), col), mine_tile
            return pltpu.make_async_remote_copy(
                src_ref=buf.at[0],
                dst_ref=buf.at[slot],
                send_sem=send.at[j],
                recv_sem=recv.at[slot],
                device_id=target,
                device_id_type=MESH,
            )

        others = [*[n_col + i for i in plane], *ring]

        def spread(buf, send, recv):
            for j in others:
                spread_copy(buf, send, recv, j).start()

        def spread_done(buf, send, recv):
            @pl.when(is_hub)
            def _():
                for j in others:
                    spread_copy(buf, send, recv, j).wait_send()

        def arrived(buf, send, recv):
            for i in range(3):
                @pl.when(not_self(i))
                def _():
                    pltpu.make_async_remote_copy(
                        src_ref=buf.at[0],
                        dst_ref=buf.at[i],
                        send_sem=send.at[1],
                        recv_sem=recv.at[i],
                        device_id=(row, over(1)),
                        device_id_type=MESH,
                    ).wait_recv()

        left = lax.broadcasted_iota(jnp.int32, (9, LANES), 1) < 64

        def pushed(tiles):
            rolled = [pltpu.roll(t, 64, axis=1) for t in tiles]
            for k in range(n_cl):
                a, b = first[k], second[k]
                own = jnp.where(a == 0, tiles[0], rolled[0])
                odd = jnp.where(b < 2, tiles[1], tiles[2])
                even = jnp.where(b < 2, rolled[1], rolled[2])
                vec = jnp.where(left, own, jnp.where((b == 1) | (b == 3), odd, even))
                vecs[k * 16 : k * 16 + 9, :] = vec
                vecs[(k + n_cl) * 16 : (k + n_cl) * 16 + 9, :] = vec
            m0 = m1 = None
            for a in range(9):
                at_obs = lane_gather(vecs[pl.ds(a, 2 * n_cl, stride=16), :], cams)
                p0, p1 = jac(0, a) * at_obs, jac(1, a) * at_obs
                m0, m1 = (p0, p1) if m0 is None else (m0 + p0, m1 + p1)
            for b in range(3):
                back = land_jac(0, b) * m0 + land_jac(1, b) * m1
                for p, part in enumerate(three_parts(back)):
                    put(bstat, p * 3 + b, part)
            for k in range(n_cl):
                put_result(k, dot_nt(of_cluster(bstat, k, 16).astype(jnp.bfloat16), one_land[k]))
            total = [result(b) + (result(3 + b) + result(6 + b)) for b in range(3)]
            return m0, m1, total, normal_solve([fac[i] for i in range(6)], *total)

        to_hubs(msg1, in1, s1, r1)

        @pl.when(is_hub)
        def _():
            total = at_hub(msg1, in1, s1, r1)
            zbuf[0, 0:8, :] = total[0:8] / total[8:16]
            zbuf[0, 8:9, :] = total[16:17] / total[17:18]
            zbuf[0, 9:17, :] = total[8:16]
            zbuf[0, 17:18, :] = total[17:18]
            spread(zbuf, s2, r2)
            zbuf[1 + row - 2 * col] = zbuf[0]

        arrived(zbuf, s2, r2)

        z_tiles = tuple(zbuf[i, 0:9, :] for i in range(3))
        m0, m1, b, y = pushed(z_tiles)
        for i in range(3):
            yvec[3 + i] = y[i]
        w0, w1 = m0, m1
        for i in range(3):
            g = lane_gather(y[i], lands)
            w0 = w0 - land_jac(0, i) * g
            w1 = w1 - land_jac(1, i) * g
        for a in range(9):
            for p, part in enumerate(three_parts(jac(0, a) * w0 + jac(1, a) * w1)):
                put(xstat, p * 8 + a if a < 8 else 24 + p, part)
        zero = jnp.zeros((16, LANES), f32)
        tiles = (zero, zero, zero)
        for k in range(n_cl):
            out = dot_nt(of_cluster(xstat, k, 32).astype(jnp.bfloat16), one_cam[k])
            out = jnp.concatenate([out[0:8] + (out[8:16] + out[16:24]), out[24:32]], axis=0)
            tiles = place(tiles, out, k)
        for i in range(3):
            t = tiles[i]
            low, high = t[0:8], t[8:9] + (t[9:10] + t[10:11])
            if i == 0:
                low = low + damp[0:8] * z_tiles[0][0:8]
                high = high + damp[8:9] * z_tiles[0][8:9]
            msg2[i, 0:8, :] = low
            msg2[i, 8:9, :] = high
        mine_tile = 1 + row - 2 * col

        def ring_copy():
            slot = lax.rem(col - hub_col + n_col, n_col)
            return pltpu.make_async_remote_copy(
                src_ref=msg2.at[0],
                dst_ref=in2.at[slot],
                send_sem=s3.at[0],
                recv_sem=r3.at[slot],
                device_id=(row, hub_col),
                device_id_type=MESH,
            )

        def plane_copy(i):
            return pltpu.make_async_remote_copy(
                src_ref=msg2.at[pl.ds(1, 2)],
                dst_ref=in3.at[i],
                send_sem=s3.at[i],
                recv_sem=r4.at[i],
                device_id=(up(i), col),
                device_id_type=MESH,
            )

        def rows_copy(i):
            return pltpu.make_async_remote_copy(
                src_ref=hsum.at[0],
                dst_ref=qbuf.at[mine_tile],
                send_sem=s4.at[i],
                recv_sem=r6.at[mine_tile],
                device_id=(up(i), col),
                device_id_type=MESH,
            )

        def total_row_copy(i):
            return pltpu.make_async_remote_copy(
                src_ref=hsum.at[1],
                dst_ref=qbuf.at[0],
                send_sem=s6.at[i],
                recv_sem=r6.at[0],
                device_id=(row, over(i)),
                device_id_type=MESH,
            )

        @pl.when(jnp.logical_not(is_hub))
        def _():
            ring_copy().start()

        for i in plane:
            plane_copy(i).start()

        @pl.when(is_hub)
        def _():
            total = msg2[0]
            for i in ring:
                pltpu.make_async_remote_copy(
                    src_ref=msg2.at[0],
                    dst_ref=in2.at[i],
                    send_sem=s3.at[0],
                    recv_sem=r3.at[i],
                    device_id=(row, over(1)),
                    device_id_type=MESH,
                ).wait_recv()
            for i in ring:
                total = total + in2[i]
            hsum[0] = total
            for i in plane:
                rows_copy(i).start()
            qbuf[mine_tile] = total

        for i in plane[::-1]:
            plane_copy(i).wait_recv()
        q1, q2 = msg2[1], msg2[2]
        for i in plane[::-1]:
            q1 = q1 + in3[i, 0]
            q2 = q2 + in3[i, 1]

        @pl.when(is_hub)
        def _():
            total = hsum[0] + jnp.where(row == 2 * col, q1, q2)
            hsum[1] = total
            for i in ring:
                total_row_copy(i).start()
            qbuf[0] = total

        for i in range(3):
            @pl.when(not_self(i))
            def _():
                pltpu.make_async_remote_copy(
                    src_ref=hsum.at[0],
                    dst_ref=qbuf.at[i],
                    send_sem=s4.at[1],
                    recv_sem=r6.at[i],
                    device_id=(row, over(1)),
                    device_id_type=MESH,
                ).wait_recv()

        q_tiles = (qbuf[0], q1 + qbuf[1], q2 + qbuf[2])
        t_tiles = tuple(q_tiles[i] / zbuf[i, 9:18, :] - z_tiles[i] for i in range(3))
        at_hub_only = jnp.where(is_hub, zbuf[0, 9:18, :], 0.0)
        own[0:1, :] = col_sum(at_hub_only * z_tiles[0] * z_tiles[0])
        own[1:2, :] = col_sum(at_hub_only * z_tiles[0] * t_tiles[0])
        own[2:3, :] = col_sum(at_hub_only * t_tiles[0] * t_tiles[0])

        m0, m1, b, y = pushed(t_tiles)
        for i in range(3):
            yvec[6 + i] = y[i]
        square = m0 * m0 + m1 * m1
        form = -0.5 * (b[0] * y[0] + b[1] * y[1] + b[2] * y[2])
        for at in range(0, dense, 8):
            form = form + square[at : at + 8]
        t = t_tiles[0]
        form = form + damp[0:8] * t[0:8] * t[0:8]
        own[3:4, :] = col_sum(form) + damp[8:9] * t[8:9] * t[8:9]

        quarter = lax.broadcasted_iota(jnp.int32, (4, LANES), 1) // 32
        which = lax.broadcasted_iota(jnp.int32, (4, LANES), 0)
        four = own[...]
        four = four + pltpu.roll(four, 64, axis=1)
        four = four + pltpu.roll(four, 32, axis=1)
        stot[0:1, :] = col_sum(jnp.where(quarter == which, four, 0.0))

        def total_copy(i, j):
            slot = i * n_col + j
            return pltpu.make_async_remote_copy(
                src_ref=stot.at[pl.ds(0, 1)],
                dst_ref=stot.at[pl.ds(slot, 1)],
                send_sem=s5,
                recv_sem=r5,
                device_id=(up(i), over(j)),
                device_id_type=MESH,
            )

        def total_wait():
            return pltpu.make_async_remote_copy(
                src_ref=stot.at[pl.ds(1, n_row * n_col - 1)],
                dst_ref=stot.at[pl.ds(1, n_row * n_col - 1)],
                send_sem=s5,
                recv_sem=r5,
                device_id=(row, over(1)),
                device_id_type=MESH,
            )

        far = sorted(
            [(i, j) for i in range(n_row) for j in range(n_col) if i or j],
            key=lambda ij: -(apart(ij[0]) + min(ij[1], n_col - ij[1]) / 2),
        )
        for i, j in far:
            total_copy(i, j).start()

        def chosen(tile, first_entry, count):
            entry = lax.broadcasted_iota(jnp.int32, (8, LANES), 1) + first_entry
            level = lax.broadcasted_iota(jnp.int32, (8, LANES), 0)
            entry = jnp.minimum(entry, 143)
            cam = entry // 9
            rest = entry - 9 * cam
            at = cam + 16 * col
            low = jnp.where(rest == level, lane_gather(tile[0:8], at), 0.0)
            high = lane_gather(jnp.broadcast_to(tile[8:9], (8, LANES)), at)
            return col_sum(low + jnp.where((rest == 8) & (level == 0), high, 0.0))[:, :count]

        z_own = jnp.concatenate([chosen(z_tiles[0], 0, 128), chosen(z_tiles[0], 128, 16)], axis=1)
        t_own = jnp.concatenate([chosen(t_tiles[0], 0, 128), chosen(t_tiles[0], 128, 16)], axis=1)

        sent_to_hubs(msg1, in1, s1, r1)
        spread_done(zbuf, s2, r2)

        @pl.when(jnp.logical_not(is_hub))
        def _():
            ring_copy().wait_send()

        for i in plane:
            plane_copy(i).wait_send()

        @pl.when(is_hub)
        def _():
            for i in plane:
                rows_copy(i).wait_send()
            for i in ring:
                total_row_copy(i).wait_send()

        total_wait().wait_recv()
        total = jnp.where(quarter == which, col_sum(stot[...]), 0.0)
        scalars = jnp.sum(total, axis=1, keepdims=True)
        rz, e, f, h = (scalars[i : i + 1] for i in range(4))
        pq = rz + e
        a0 = rz / pq
        new = a0 * ((rz * f - e * e) / pq)
        g = e / pq + new / rz
        curve = g * g * pq - 2.0 * g * a0 * (e + f) + a0 * a0 * h
        a1 = new / curve
        big_a = a0 + a1 * g
        big_b = -a1 * a0
        cam_ref[...] = big_a * z_own + big_b * t_own
        for b in range(3):
            land = -(yvec[b] + big_a * yvec[3 + b] + big_b * yvec[6 + b])
            land_ref[b] = land[0:n_cl]
        total_wait().wait_send()

    return kernel


def write_out(cam_ref, land_ref, cam_out, land_out, sem):
    copies = (
        pltpu.make_async_copy(cam_ref, cam_out, sem.at[0]),
        pltpu.make_async_copy(land_ref, land_out, sem.at[1]),
    )
    for copy in copies:
        copy.start()
    for copy in copies:
        copy.wait()


def per_device(cam_jac, land_jac, resid, obs_cam, obs_land, pairs, cam_damp):
    n_row = lax.axis_size("row")
    n_col = lax.axis_size("col")
    n_cl, _, n_obs = cam_jac.shape
    shard = cam_damp.shape[0]
    f32 = jnp.float32
    slots = n_row + n_col
    tiles = n_obs // LANES
    dense = n_cl * tiles
    vmem = pl.BlockSpec(memory_space=pltpu.VMEM)
    dma = pltpu.SemaphoreType.DMA

    def entries_first(x):
        return (
            x.reshape(n_cl, -1, tiles, LANES).transpose(1, 2, 0, 3).reshape(-1, LANES)
        )

    cam, land = pl.pallas_call(
        make_kernel(n_row, n_col, n_cl, n_obs),
        out_shape=(
            jax.ShapeDtypeStruct((1, shard), f32),
            jax.ShapeDtypeStruct((3, n_cl, LANES), f32),
        ),
        in_specs=[pl.BlockSpec(memory_space=pltpu.HBM)] * 7,
        out_specs=(vmem, vmem),
        scratch_shapes=[
            pltpu.SMEM((2, n_cl), jnp.int32),
            pltpu.VMEM((18 * dense, LANES), f32),
            pltpu.VMEM((6 * dense, LANES), f32),
            pltpu.VMEM((2 * dense, LANES), f32),
            pltpu.VMEM((dense, LANES), jnp.int32),
            pltpu.VMEM((dense, LANES), jnp.int32),
            pltpu.VMEM((1, shard), f32),
            dma((7,)),
            pltpu.VMEM((n_cl, LANES, n_obs), jnp.bfloat16),
            pltpu.VMEM((n_cl, LANES, n_obs), jnp.bfloat16),
            pltpu.VMEM((32 * dense, LANES), f32),
            pltpu.VMEM((24 * dense, LANES), f32),
            pltpu.VMEM((32 * dense, LANES), f32),
            pltpu.VMEM((16 * dense, LANES), f32),
            pltpu.VMEM((2 * n_cl * 32, LANES), f32),
            pltpu.VMEM((2 * n_cl * 16, LANES), f32),
            pltpu.VMEM((6, 8, LANES), f32),
            pltpu.VMEM((9, 8, LANES), f32),
            pltpu.VMEM((3, 18, LANES), f32),
            pltpu.VMEM((3, 9, LANES), f32),
            pltpu.VMEM((slots, 18, LANES), f32),
            pltpu.VMEM((3, 18, LANES), f32),
            pltpu.VMEM((n_col, 9, LANES), f32),
            pltpu.VMEM((n_row, 2, 9, LANES), f32),
            pltpu.VMEM((2, 9, LANES), f32),
            pltpu.VMEM((3, 9, LANES), f32),
            pltpu.VMEM((4, LANES), f32),
            pltpu.VMEM((n_row * n_col, LANES), f32),
            dma((3,)), dma((slots,)),
            dma((slots,)), dma((3,)),
            dma((n_row,)), dma((n_col,)),
            dma((n_row,)), dma((n_row,)),
            dma, dma,
            dma((n_col,)), dma((3,)),
        ],
        compiler_params=pltpu.CompilerParams(collective_id=0, has_side_effects=True, vmem_limit_bytes=VMEM),
        name="schur_step",
    )(
        *(
            pltpu.with_memory_space_constraint(x, pltpu.HBM)
            for x in (
        pairs.T,
        entries_first(cam_jac),
        entries_first(land_jac),
        resid.reshape(n_cl, 2, tiles, LANES).transpose(0, 2, 1, 3).reshape(-1, LANES),
        obs_cam.reshape(n_cl, tiles, LANES).transpose(1, 0, 2).reshape(-1, LANES),
        obs_land.reshape(n_cl, tiles, LANES).transpose(1, 0, 2).reshape(-1, LANES),
        cam_damp.reshape(1, shard),
            )
        )
    )
    cam, land = pl.pallas_call(
        write_out,
        out_shape=(
            jax.ShapeDtypeStruct((1, shard), f32),
            jax.ShapeDtypeStruct((3, n_cl, LANES), f32),
        ),
        in_specs=[vmem] * 2,
        out_specs=[pl.BlockSpec(memory_space=pltpu.HBM)] * 2,
        scratch_shapes=[dma((2,))],
        compiler_params=pltpu.CompilerParams(vmem_limit_bytes=1 << 20),
        name="write_out",
    )(cam, land)
    return cam.reshape(shard), land.transpose(1, 0, 2)


def solution(mesh):
    in_specs = (
        P(("row", "col"), None, None),
        P(("row", "col"), None, None),
        P(("row", "col"), None, None),
        P(("row", "col"), None),
        P(("row", "col"), None),
        P(("row", "col"), None),
        P(("row", "col")),
    )
    out_specs = (P(("row", "col")), P(("row", "col"), None, None))
    return jax.shard_map(
        per_device, mesh=mesh, in_specs=in_specs, out_specs=out_specs, check_vma=False
    )
```

```python
import jax
import jax.numpy as jnp
from jax import lax
from jax.experimental import pallas as pl
from jax.experimental.pallas import tpu as pltpu
from jax.sharding import PartitionSpec as P

DAMPING = 1.0
MESH = pl.DeviceIdType.MESH
LANES = 128
SIDE = 4
VMEM = 8 << 20


def lane_gather(table, index):
    dims = lax.GatherDimensionNumbers((), (1,), (1,), (0,), (0,))
    pieces = [
        lax.gather(
            table,
            index[at : at + 8, :, None],
            dims,
            slice_sizes=(1, 1),
            mode=lax.GatherScatterMode.PROMISE_IN_BOUNDS,
        )
        for at in range(0, index.shape[0], 8)
    ]
    return pieces[0] if len(pieces) == 1 else jnp.concatenate(pieces, axis=0)


def three_parts(x):
    high = x.astype(jnp.bfloat16).astype(jnp.float32)
    rest = x - high
    mid = rest.astype(jnp.bfloat16).astype(jnp.float32)
    return high, mid, rest - mid


def dot_nt(x, onehot):
    return lax.dot_general(
        x, onehot, (((1,), (1,)), ((), ())), preferred_element_type=jnp.float32
    )


def stacked_parts(x):
    high = x.astype(jnp.bfloat16)
    rest = x - high.astype(jnp.float32)
    mid = rest.astype(jnp.bfloat16)
    low = (rest - mid.astype(jnp.float32)).astype(jnp.bfloat16)
    return jnp.concatenate([high, mid, low], axis=0)


def add_parts(out):
    rows = out.shape[0] // 3
    return out[:rows] + (out[rows : 2 * rows] + out[2 * rows :])


def col_sum(x):
    return jnp.sum(x, axis=0, keepdims=True)


def lower_solve(f, a, b, c):
    one = a * f[0]
    two = (b - f[1] * one) * f[3]
    three = (c - f[2] * one - f[4] * two) * f[5]
    return one, two, three


def upper_solve(f, a, b, c):
    three = c * f[5]
    two = (b - f[4] * three) * f[3]
    one = (a - f[1] * two - f[2] * three) * f[0]
    return one, two, three


def normal_solve(f, a, b, c):
    return upper_solve(f, *lower_solve(f, a, b, c))


def cholesky_three(v):
    inv_first = 1.0 / jnp.sqrt(v[0])
    low_one = v[1] * inv_first
    low_two = v[2] * inv_first
    inv_second = 1.0 / jnp.sqrt(v[3] - low_one * low_one)
    low_three = (v[4] - low_two * low_one) * inv_second
    inv_third = 1.0 / jnp.sqrt(v[5] - low_two * low_two - low_three * low_three)
    return inv_first, low_one, low_two, inv_second, low_three, inv_third


def make_kernel(n_row, n_col, n_cl, n_obs):
    f32 = jnp.float32

    tiles_n = n_obs // LANES
    dense = tiles_n * n_cl

    def kernel(
        pairs_in, cj_in, lj_in, re_in, oc_in, ol_in, damp_in,
        cam_ref, land_ref,
        pairs_ref, cj_ref, lj_ref, re_ref, oc_ref, ol_ref, damp_ref, s0,
        one_cam, one_land, ustat, wstat, xstat, bstat, res, vecs, fac, yvec,
        msg1, msg2, in1, zbuf, in2, in3, in4, in5, qbuf, own, stot,
        s1, r1, s2, r2, s3, r3, s4, r4, s5, r5, s6, r6, s7, r7,
    ):
        one = jnp.asarray(1, jnp.bfloat16)
        nil = jnp.asarray(0, jnp.bfloat16)
        row = lax.axis_index("row")
        col = lax.axis_index("col")
        hub_col = row // 2
        is_hub = col == hub_col
        z, x = row // SIDE, lax.rem(row, SIDE)
        zs = [lax.rem(z + d, SIDE) * SIDE for d in range(SIDE)]
        xs = [lax.rem(x + d, SIDE) for d in range(SIDE)]
        cols = [lax.rem(col + d, n_col) for d in range(n_col)]
        up = lambda i: zs[i // SIDE] + xs[i % SIDE]
        over = lambda i: cols[i]

        def apart(i):
            return sum(min(d, SIDE - d) for d in (i // SIDE, i % SIDE))

        plane = sorted(range(1, n_row), key=lambda i: -apart(i))
        ring = [*range(2, n_col - 1), 1, n_col - 1]

        loads = [
            pltpu.make_async_copy(source, target, s0.at[n])
            for n, (source, target) in enumerate(
                (
                    (oc_in, oc_ref),
                    (ol_in, ol_ref),
                    (lj_in, lj_ref),
                    (re_in, re_ref),
                    (cj_in, cj_ref),
                    (pairs_in, pairs_ref),
                    (damp_in, damp_ref),
                )
            )
        ]
        for load in loads:
            load.start()

        barrier = pltpu.get_barrier_semaphore()

        @pl.when(is_hub)
        def _():
            for i in plane:
                pl.semaphore_signal(barrier, inc=1, device_id=(up(i), col), device_id_type=MESH)
            for i in range(1, n_col):
                pl.semaphore_signal(barrier, inc=1, device_id=(row, over(i)), device_id_type=MESH)

        def place(tiles, out, k):
            rolled = pltpu.roll(out, 64, axis=1)
            half = lax.broadcasted_iota(jnp.int32, out.shape, 1) < 64

            def pick(cond, x):
                return jnp.where(cond, x, 0.0)

            a, b = first[k], second[k]
            return (
                tiles[0] + jnp.where(half, pick(a == 0, out), pick(a == 1, rolled)),
                tiles[1] + jnp.where(half, pick(b == 0, rolled), pick(b == 1, out)),
                tiles[2] + jnp.where(half, pick(b == 2, rolled), pick(b == 3, out)),
            )

        def jac(r, a):
            return cj_ref[(r * 9 + a) * dense : (r * 9 + a + 1) * dense, :]

        def land_jac(r, b):
            return lj_ref[(r * 3 + b) * dense : (r * 3 + b + 1) * dense, :]

        def put(ref, q, value):
            ref[q * dense : (q + 1) * dense, :] = value

        def of_cluster(ref, k, rows):
            return jnp.concatenate(
                [ref[pl.ds(j * n_cl + k, rows, stride=dense), :] for j in range(tiles_n)], axis=1
            )

        def put_result(k, value):
            rows = value.shape[0]
            res[k * 32 : k * 32 + rows, :] = value
            res[(k + n_cl) * 32 : (k + n_cl) * 32 + rows, :] = value

        def result(q):
            return res[pl.ds(q, 2 * n_cl, stride=32), :]

        loads[0].wait()
        loads[1].wait()
        cams = oc_ref[...]
        lands = ol_ref[...]

        cams_f = cams.astype(f32)
        lands_f = lands.astype(f32)

        def packed_row(x, j, k):
            at = j * n_cl + k
            return jnp.broadcast_to(x[at : at + 1, :], (16, LANES)).astype(jnp.bfloat16)

        level = [
            (lax.broadcasted_iota(jnp.int32, (16, LANES), 0) + 16 * i).astype(f32).astype(jnp.bfloat16)
            for i in range(8)
        ]
        for k in range(n_cl):
            for j in range(tiles_n):
                land_row = packed_row(lands_f, j, k)
                cam_row = packed_row(cams_f, j, k)
                for i in range(8):
                    at = (k, slice(16 * i, 16 * i + 16), slice(j * LANES, (j + 1) * LANES))
                    one_land[at] = jnp.where(level[i] == land_row, one, nil)
                    one_cam[at] = jnp.where(level[i] == cam_row, one, nil)

        power = jnp.full((dense, LANES), 2.0**-64, f32)
        for i in range(7):
            power = power * jnp.where(((cams >> i) & 1) == 1, 2.0 ** (2**i), 1.0)
        code = power * (1.0 + lands_f * (1.0 / 128.0))
        code_t = code.T

        zero = jnp.zeros((dense, LANES), f32)
        for q in range(27, 32):
            put(xstat, q, zero)
            put(ustat, q, zero)
        for q in range(18, 24):
            put(wstat, q, zero)
        for q in range(9, 16):
            put(bstat, q, zero)
        loads[2].wait()
        loads[3].wait()
        ka = [land_jac(0, b) for b in range(3)]
        kb = [land_jac(1, b) for b in range(3)]
        e0, e1 = (
            jnp.concatenate(
                [re_ref[pl.ds(2 * j + r, n_cl, stride=2 * tiles_n), :] for j in range(tiles_n)], axis=0
            )
            for r in range(2)
        )
        stats = [
            ka[i] * ka[j] + kb[i] * kb[j]
            for i, j in ((0, 0), (0, 1), (0, 2), (1, 1), (1, 2), (2, 2))
        ] + [ka[b] * e0 + kb[b] * e1 for b in range(3)]
        for q, stat in enumerate(stats):
            for p, part in enumerate(three_parts(stat)):
                put(xstat, p * 9 + q, part)
        for k in range(n_cl):
            put_result(k, dot_nt(of_cluster(xstat, k, 32).astype(jnp.bfloat16), one_land[k]))
        v = [result(q) + (result(9 + q) + result(18 + q)) for q in range(9)]
        v[0], v[3], v[5] = v[0] + DAMPING, v[3] + DAMPING, v[5] + DAMPING
        factor = cholesky_three(v[:6])
        base = normal_solve(factor, v[6], v[7], v[8])
        for i in range(6):
            fac[i] = factor[i]
        for b in range(3):
            yvec[b] = base[b]

        loads[4].wait()
        loads[5].wait()
        loads[6].wait()
        first = [pairs_ref[0, k] - 2 * row for k in range(n_cl)]
        second = [pairs_ref[1, k] - 4 * col for k in range(n_cl)]

        lane = lax.broadcasted_iota(jnp.int32, (16, LANES), 1)
        sub = lax.broadcasted_iota(jnp.int32, (16, LANES), 0)
        flat = (lane - 16 * col) * 9 + sub
        mine = (lane >= 16 * col) & (lane < 16 * col + 16) & (sub < 9)
        flat = jnp.where(mine, flat, 0)
        damp_low = jnp.broadcast_to(damp_ref[:, :LANES], (8, LANES))
        damp_high = jnp.broadcast_to(
            jnp.concatenate([damp_ref[:, LANES:], jnp.zeros((1, 2 * LANES - 144), f32)], axis=1),
            (8, LANES),
        )
        damp = jnp.where(
            flat < LANES,
            lane_gather(damp_low, jnp.minimum(flat, LANES - 1)),
            lane_gather(damp_high, jnp.maximum(flat - LANES, 0)),
        )
        damp = jnp.where(mine, damp, 0.0)

        f = [lane_gather(factor[i], lands) for i in range(6)]
        g = [lane_gather(base[b], lands) for b in range(3)]
        w0 = ka[0] * g[0] + ka[1] * g[1] + ka[2] * g[2] - e0
        w1 = kb[0] * g[0] + kb[1] * g[1] + kb[2] * g[2] - e1
        for a in range(9):
            j0, j1 = jac(0, a), jac(1, a)
            solved = lower_solve(f, *[j0 * ka[b] + j1 * kb[b] for b in range(3)])
            for b in range(3):
                put(ustat, b * 8 + a if a < 8 else 24 + b, solved[b])
            put(wstat, a if a < 8 else 16, j0 * w0 + j1 * w1)
            put(wstat, 8 + a if a < 8 else 17, j0 * j0 + j1 * j1)
        zero = jnp.zeros((32, LANES), f32)
        tiles = (zero, zero, zero)
        for k in range(n_cl):
            rows_packed = [
                jnp.concatenate([packed_row(code, j, k)] * 8, axis=0) for j in range(tiles_n)
            ]
            blocks = []
            for j in range(tiles_n):
                at = j * n_cl + k
                column = jnp.broadcast_to(code_t[:, at : at + 1], (LANES, LANES)).astype(jnp.bfloat16)
                blocks.append(
                    jnp.concatenate([jnp.where(column == r, one, nil) for r in rows_packed], axis=1)
                )
            match = jnp.concatenate(blocks, axis=0)
            solved = of_cluster(ustat, k, 32)
            paired = add_parts(
                jnp.dot(stacked_parts(solved), match, preferred_element_type=jnp.float32)
            )
            square = solved * paired
            plain = of_cluster(wstat, k, 24)
            diag = plain[8:16] - (square[0:8] + square[8:16] + square[16:24])
            lhs = jnp.concatenate([plain[0:8], diag, plain[16:24], square[24:32]], axis=0)
            tiles = place(tiles, add_parts(dot_nt(stacked_parts(lhs), one_cam[k])), k)
        for i in range(3):
            extra = damp if i == 0 else jnp.zeros((16, LANES), f32)
            t = tiles[i]
            msg1[i, 0:8, :] = t[0:8]
            msg1[i, 8:16, :] = t[8:16] + extra[0:8]
            msg1[i, 16:17, :] = t[16:17]
            msg1[i, 17:18, :] = t[17:18] - (t[24:25] + t[25:26] + t[26:27]) + extra[8:9]

        pl.semaphore_wait(barrier, jnp.where(is_hub, 1, 3))

        hub_of = ((row, hub_col), (2 * col, col), (2 * col + 1, col))

        def contribution(msg, buf, send, recv, i):
            row_slot = lax.rem(col - hub_col + n_col, n_col)
            hub_z, hub_x = (2 * col + i - 1) // SIDE, lax.rem(2 * col + i - 1, SIDE)
            plane_slot = lax.rem(z - hub_z + SIDE, SIDE) * SIDE + lax.rem(x - hub_x + SIDE, SIDE)
            slot = row_slot if i == 0 else n_col + plane_slot
            return pltpu.make_async_remote_copy(
                src_ref=msg.at[i],
                dst_ref=buf.at[slot],
                send_sem=send.at[i],
                recv_sem=recv.at[slot],
                device_id=hub_of[i],
                device_id_type=MESH,
            )

        def not_self(i):
            return jnp.logical_not(is_hub) if i == 0 else row != 2 * col + (i - 1)

        def to_hubs(msg, buf, send, recv):
            for i in range(3):
                @pl.when(not_self(i))
                def _():
                    contribution(msg, buf, send, recv, i).start()

        def sent_to_hubs(msg, buf, send, recv):
            for i in range(3):
                @pl.when(not_self(i))
                def _():
                    contribution(msg, buf, send, recv, i).wait_send()

        def at_hub(msg, buf, send, recv):
            mine_tile = 1 + row - 2 * col
            total = msg[0] + msg[mine_tile]
            late = [n_col + i for i in plane[::-1]]
            for slot in [*ring, *late]:
                pltpu.make_async_remote_copy(
                    src_ref=msg.at[0],
                    dst_ref=buf.at[slot],
                    send_sem=send.at[0],
                    recv_sem=recv.at[slot],
                    device_id=(row, over(1)),
                    device_id_type=MESH,
                ).wait_recv()
            for slot in [*ring, *late]:
                total = total + buf[slot]
            return total

        def spread_copy(buf, send, recv, j):
            mine_tile = 1 + row - 2 * col
            if j < n_col:
                target, slot = (row, over(j)), 0
            else:
                target, slot = (up(j - n_col), col), mine_tile
            return pltpu.make_async_remote_copy(
                src_ref=buf.at[0],
                dst_ref=buf.at[slot],
                send_sem=send.at[j],
                recv_sem=recv.at[slot],
                device_id=target,
                device_id_type=MESH,
            )

        others = [*[n_col + i for i in plane], *ring]

        def spread(buf, send, recv):
            for j in others:
                spread_copy(buf, send, recv, j).start()

        def spread_done(buf, send, recv):
            @pl.when(is_hub)
            def _():
                for j in others:
                    spread_copy(buf, send, recv, j).wait_send()

        def arrived(buf, send, recv):
            for i in range(3):
                @pl.when(not_self(i))
                def _():
                    pltpu.make_async_remote_copy(
                        src_ref=buf.at[0],
                        dst_ref=buf.at[i],
                        send_sem=send.at[1],
                        recv_sem=recv.at[i],
                        device_id=(row, over(1)),
                        device_id_type=MESH,
                    ).wait_recv()

        left = lax.broadcasted_iota(jnp.int32, (9, LANES), 1) < 64

        def pushed(tiles):
            rolled = [pltpu.roll(t, 64, axis=1) for t in tiles]
            for k in range(n_cl):
                a, b = first[k], second[k]
                own = jnp.where(a == 0, tiles[0], rolled[0])
                odd = jnp.where(b < 2, tiles[1], tiles[2])
                even = jnp.where(b < 2, rolled[1], rolled[2])
                vec = jnp.where(left, own, jnp.where((b == 1) | (b == 3), odd, even))
                vecs[k * 16 : k * 16 + 9, :] = vec
                vecs[(k + n_cl) * 16 : (k + n_cl) * 16 + 9, :] = vec
            m0 = m1 = None
            for a in range(9):
                at_obs = lane_gather(vecs[pl.ds(a, 2 * n_cl, stride=16), :], cams)
                p0, p1 = jac(0, a) * at_obs, jac(1, a) * at_obs
                m0, m1 = (p0, p1) if m0 is None else (m0 + p0, m1 + p1)
            for b in range(3):
                back = land_jac(0, b) * m0 + land_jac(1, b) * m1
                for p, part in enumerate(three_parts(back)):
                    put(bstat, p * 3 + b, part)
            for k in range(n_cl):
                put_result(k, dot_nt(of_cluster(bstat, k, 16).astype(jnp.bfloat16), one_land[k]))
            total = [result(b) + (result(3 + b) + result(6 + b)) for b in range(3)]
            return m0, m1, total, normal_solve([fac[i] for i in range(6)], *total)

        to_hubs(msg1, in1, s1, r1)

        @pl.when(is_hub)
        def _():
            total = at_hub(msg1, in1, s1, r1)
            zbuf[0, 0:8, :] = total[0:8] / total[8:16]
            zbuf[0, 8:9, :] = total[16:17] / total[17:18]
            zbuf[0, 9:17, :] = total[8:16]
            zbuf[0, 17:18, :] = total[17:18]
            spread(zbuf, s2, r2)
            zbuf[1 + row - 2 * col] = zbuf[0]

        arrived(zbuf, s2, r2)

        z_tiles = tuple(zbuf[i, 0:9, :] for i in range(3))
        m0, m1, b, y = pushed(z_tiles)
        for i in range(3):
            yvec[3 + i] = y[i]
        w0, w1 = m0, m1
        for i in range(3):
            g = lane_gather(y[i], lands)
            w0 = w0 - land_jac(0, i) * g
            w1 = w1 - land_jac(1, i) * g
        for a in range(9):
            for p, part in enumerate(three_parts(jac(0, a) * w0 + jac(1, a) * w1)):
                put(xstat, p * 8 + a if a < 8 else 24 + p, part)
        zero = jnp.zeros((16, LANES), f32)
        tiles = (zero, zero, zero)
        for k in range(n_cl):
            out = dot_nt(of_cluster(xstat, k, 32).astype(jnp.bfloat16), one_cam[k])
            out = jnp.concatenate([out[0:8] + (out[8:16] + out[16:24]), out[24:32]], axis=0)
            tiles = place(tiles, out, k)
        for i in range(3):
            t = tiles[i]
            low, high = t[0:8], t[8:9] + (t[9:10] + t[10:11])
            if i == 0:
                low = low + damp[0:8] * z_tiles[0][0:8]
                high = high + damp[8:9] * z_tiles[0][8:9]
            msg2[i, 0:8, :] = low
            msg2[i, 8:9, :] = high
        parity = lax.rem(row, 2)

        def send(source, target_ref, send_sem, recv_sem, device):
            return pltpu.make_async_remote_copy(
                src_ref=source,
                dst_ref=target_ref,
                send_sem=send_sem,
                recv_sem=recv_sem,
                device_id=device,
                device_id_type=MESH,
            )

        def ring_copy(i):
            return send(msg2.at[0], in2.at[i], s3.at[i], r3.at[i], (row, over(i)))

        def plane_copy(i):
            return send(msg2.at[pl.ds(1, 2)], in3.at[i], s4.at[i], r4.at[i], (up(i), col))

        def row_copy(i):
            slot = parity * n_col + col
            return send(msg2.at[0], in4.at[slot], s6.at[i], r6.at[slot], (up(i), hub_col))

        def col_copy(j, i):
            at = j * n_col + i
            return send(msg2.at[1 + j], in5.at[row], s7.at[at], r7.at[row], (2 * col + j, over(i)))

        sends = [
            *[row_copy(i) for i in plane if apart(i) > 2],
            *[col_copy(j, i) for i in ring[:-2] for j in range(2)],
            *[row_copy(i) for i in plane if apart(i) <= 2],
            *[col_copy(j, i) for i in ring[-2:] for j in range(2)],
            *[plane_copy(i) for i in plane],
            *[ring_copy(i) for i in ring],
        ]
        for copy in sends:
            copy.start()

        for i in ring:
            ring_copy(i).wait_recv()
        q_row = msg2[0]
        for i in ring:
            q_row = q_row + in2[i]
        for i in plane[::-1]:
            plane_copy(i).wait_recv()
        q_col = [msg2[1], msg2[2]]
        for i in plane[::-1]:
            q_col = [q_col[j] + in3[i, j] for j in range(2)]

        @pl.when(jnp.logical_not(is_hub))
        def _():
            for i in range(n_row):
                send(msg2.at[0], in5.at[i], s7.at[1], r7.at[i], (row, over(1))).wait_recv()
            total = in5[0]
            for i in range(1, n_row):
                total = total + in5[i]
            qbuf[0] = total

        @pl.when(is_hub)
        def _():
            qbuf[0] = jnp.where(row == 2 * col, q_col[0], q_col[1])

        for j in range(2):
            @pl.when(row != 2 * col + j)
            def _():
                for i in range(n_col):
                    at = j * n_col + i
                    send(msg2.at[0], in4.at[at], s6.at[1], r6.at[at], (row, over(1))).wait_recv()
                total = in4[j * n_col]
                for i in range(1, n_col):
                    total = total + in4[j * n_col + i]
                qbuf[1 + j] = total

            @pl.when(row == 2 * col + j)
            def _():
                qbuf[1 + j] = q_row

        q_tiles = (q_row + qbuf[0], q_col[0] + qbuf[1], q_col[1] + qbuf[2])
        t_tiles = tuple(q_tiles[i] / zbuf[i, 9:18, :] - z_tiles[i] for i in range(3))
        at_hub_only = jnp.where(is_hub, zbuf[0, 9:18, :], 0.0)
        own[0:1, :] = col_sum(at_hub_only * z_tiles[0] * z_tiles[0])
        own[1:2, :] = col_sum(at_hub_only * z_tiles[0] * t_tiles[0])
        own[2:3, :] = col_sum(at_hub_only * t_tiles[0] * t_tiles[0])

        m0, m1, b, y = pushed(t_tiles)
        for i in range(3):
            yvec[6 + i] = y[i]
        square = m0 * m0 + m1 * m1
        form = -0.5 * (b[0] * y[0] + b[1] * y[1] + b[2] * y[2])
        for at in range(0, dense, 8):
            form = form + square[at : at + 8]
        t = t_tiles[0]
        form = form + damp[0:8] * t[0:8] * t[0:8]
        own[3:4, :] = col_sum(form) + damp[8:9] * t[8:9] * t[8:9]

        quarter = lax.broadcasted_iota(jnp.int32, (4, LANES), 1) // 32
        which = lax.broadcasted_iota(jnp.int32, (4, LANES), 0)
        four = own[...]
        four = four + pltpu.roll(four, 64, axis=1)
        four = four + pltpu.roll(four, 32, axis=1)
        stot[0:1, :] = col_sum(jnp.where(quarter == which, four, 0.0))

        def total_copy(i, j):
            slot = i * n_col + j
            return pltpu.make_async_remote_copy(
                src_ref=stot.at[pl.ds(0, 1)],
                dst_ref=stot.at[pl.ds(slot, 1)],
                send_sem=s5,
                recv_sem=r5,
                device_id=(up(i), over(j)),
                device_id_type=MESH,
            )

        def total_wait():
            return pltpu.make_async_remote_copy(
                src_ref=stot.at[pl.ds(1, n_row * n_col - 1)],
                dst_ref=stot.at[pl.ds(1, n_row * n_col - 1)],
                send_sem=s5,
                recv_sem=r5,
                device_id=(row, over(1)),
                device_id_type=MESH,
            )

        far = sorted(
            [(i, j) for i in range(n_row) for j in range(n_col) if i or j],
            key=lambda ij: -(apart(ij[0]) + min(ij[1], n_col - ij[1]) / 2),
        )
        for i, j in far:
            total_copy(i, j).start()

        def chosen(tile, first_entry, count):
            entry = lax.broadcasted_iota(jnp.int32, (8, LANES), 1) + first_entry
            level = lax.broadcasted_iota(jnp.int32, (8, LANES), 0)
            entry = jnp.minimum(entry, 143)
            cam = entry // 9
            rest = entry - 9 * cam
            at = cam + 16 * col
            low = jnp.where(rest == level, lane_gather(tile[0:8], at), 0.0)
            high = lane_gather(jnp.broadcast_to(tile[8:9], (8, LANES)), at)
            return col_sum(low + jnp.where((rest == 8) & (level == 0), high, 0.0))[:, :count]

        z_own = jnp.concatenate([chosen(z_tiles[0], 0, 128), chosen(z_tiles[0], 128, 16)], axis=1)
        t_own = jnp.concatenate([chosen(t_tiles[0], 0, 128), chosen(t_tiles[0], 128, 16)], axis=1)

        sent_to_hubs(msg1, in1, s1, r1)
        spread_done(zbuf, s2, r2)

        for copy in sends:
            copy.wait_send()

        total_wait().wait_recv()
        total = jnp.where(quarter == which, col_sum(stot[...]), 0.0)
        scalars = jnp.sum(total, axis=1, keepdims=True)
        rz, e, f, h = (scalars[i : i + 1] for i in range(4))
        pq = rz + e
        a0 = rz / pq
        new = a0 * ((rz * f - e * e) / pq)
        g = e / pq + new / rz
        curve = g * g * pq - 2.0 * g * a0 * (e + f) + a0 * a0 * h
        a1 = new / curve
        big_a = a0 + a1 * g
        big_b = -a1 * a0
        cam_ref[...] = big_a * z_own + big_b * t_own
        for b in range(3):
            land = -(yvec[b] + big_a * yvec[3 + b] + big_b * yvec[6 + b])
            land_ref[b] = land[0:n_cl]
        total_wait().wait_send()

    return kernel


def write_out(cam_ref, land_ref, cam_out, land_out, sem):
    copies = (
        pltpu.make_async_copy(cam_ref, cam_out, sem.at[0]),
        pltpu.make_async_copy(land_ref, land_out, sem.at[1]),
    )
    for copy in copies:
        copy.start()
    for copy in copies:
        copy.wait()


def per_device(cam_jac, land_jac, resid, obs_cam, obs_land, pairs, cam_damp):
    n_row = lax.axis_size("row")
    n_col = lax.axis_size("col")
    n_cl, _, n_obs = cam_jac.shape
    shard = cam_damp.shape[0]
    f32 = jnp.float32
    slots = n_row + n_col
    tiles = n_obs // LANES
    dense = n_cl * tiles
    vmem = pl.BlockSpec(memory_space=pltpu.VMEM)
    dma = pltpu.SemaphoreType.DMA

    def entries_first(x):
        return (
            x.reshape(n_cl, -1, tiles, LANES).transpose(1, 2, 0, 3).reshape(-1, LANES)
        )

    cam, land = pl.pallas_call(
        make_kernel(n_row, n_col, n_cl, n_obs),
        out_shape=(
            jax.ShapeDtypeStruct((1, shard), f32),
            jax.ShapeDtypeStruct((3, n_cl, LANES), f32),
        ),
        in_specs=[pl.BlockSpec(memory_space=pltpu.HBM)] * 7,
        out_specs=(vmem, vmem),
        scratch_shapes=[
            pltpu.SMEM((2, n_cl), jnp.int32),
            pltpu.VMEM((18 * dense, LANES), f32),
            pltpu.VMEM((6 * dense, LANES), f32),
            pltpu.VMEM((2 * dense, LANES), f32),
            pltpu.VMEM((dense, LANES), jnp.int32),
            pltpu.VMEM((dense, LANES), jnp.int32),
            pltpu.VMEM((1, shard), f32),
            dma((7,)),
            pltpu.VMEM((n_cl, LANES, n_obs), jnp.bfloat16),
            pltpu.VMEM((n_cl, LANES, n_obs), jnp.bfloat16),
            pltpu.VMEM((32 * dense, LANES), f32),
            pltpu.VMEM((24 * dense, LANES), f32),
            pltpu.VMEM((32 * dense, LANES), f32),
            pltpu.VMEM((16 * dense, LANES), f32),
            pltpu.VMEM((2 * n_cl * 32, LANES), f32),
            pltpu.VMEM((2 * n_cl * 16, LANES), f32),
            pltpu.VMEM((6, 8, LANES), f32),
            pltpu.VMEM((9, 8, LANES), f32),
            pltpu.VMEM((3, 18, LANES), f32),
            pltpu.VMEM((3, 9, LANES), f32),
            pltpu.VMEM((slots, 18, LANES), f32),
            pltpu.VMEM((3, 18, LANES), f32),
            pltpu.VMEM((n_col, 9, LANES), f32),
            pltpu.VMEM((n_row, 2, 9, LANES), f32),
            pltpu.VMEM((2 * n_col, 9, LANES), f32),
            pltpu.VMEM((n_row, 9, LANES), f32),
            pltpu.VMEM((3, 9, LANES), f32),
            pltpu.VMEM((4, LANES), f32),
            pltpu.VMEM((n_row * n_col, LANES), f32),
            dma((3,)), dma((slots,)),
            dma((slots,)), dma((3,)),
            dma((n_col,)), dma((n_col,)),
            dma((n_row,)), dma((n_row,)),
            dma, dma,
            dma((n_row,)), dma((2 * n_col,)),
            dma((2 * n_col,)), dma((n_row,)),
        ],
        compiler_params=pltpu.CompilerParams(collective_id=0, has_side_effects=True, vmem_limit_bytes=VMEM),
        name="schur_step",
    )(
        *(
            pltpu.with_memory_space_constraint(x, pltpu.HBM)
            for x in (
        pairs.T,
        entries_first(cam_jac),
        entries_first(land_jac),
        resid.reshape(n_cl, 2, tiles, LANES).transpose(0, 2, 1, 3).reshape(-1, LANES),
        obs_cam.reshape(n_cl, tiles, LANES).transpose(1, 0, 2).reshape(-1, LANES),
        obs_land.reshape(n_cl, tiles, LANES).transpose(1, 0, 2).reshape(-1, LANES),
        cam_damp.reshape(1, shard),
            )
        )
    )
    cam, land = pl.pallas_call(
        write_out,
        out_shape=(
            jax.ShapeDtypeStruct((1, shard), f32),
            jax.ShapeDtypeStruct((3, n_cl, LANES), f32),
        ),
        in_specs=[vmem] * 2,
        out_specs=[pl.BlockSpec(memory_space=pltpu.HBM)] * 2,
        scratch_shapes=[dma((2,))],
        compiler_params=pltpu.CompilerParams(vmem_limit_bytes=1 << 20),
        name="write_out",
    )(cam, land)
    return cam.reshape(shard), land.transpose(1, 0, 2)


def solution(mesh):
    in_specs = (
        P(("row", "col"), None, None),
        P(("row", "col"), None, None),
        P(("row", "col"), None, None),
        P(("row", "col"), None),
        P(("row", "col"), None),
        P(("row", "col"), None),
        P(("row", "col")),
    )
    out_specs = (P(("row", "col")), P(("row", "col"), None, None))
    return jax.shard_map(
        per_device, mesh=mesh, in_specs=in_specs, out_specs=out_specs, check_vma=False
    )
```

```python
import jax
import jax.numpy as jnp
from jax import lax
from jax.experimental import pallas as pl
from jax.experimental.pallas import tpu as pltpu
from jax.sharding import PartitionSpec as P

DAMPING = 1.0
MESH = pl.DeviceIdType.MESH
LANES = 128
SIDE = 4
VMEM = 8 << 20


def lane_gather(table, index):
    dims = lax.GatherDimensionNumbers((), (1,), (1,), (0,), (0,))
    pieces = [
        lax.gather(
            table,
            index[at : at + 8, :, None],
            dims,
            slice_sizes=(1, 1),
            mode=lax.GatherScatterMode.PROMISE_IN_BOUNDS,
        )
        for at in range(0, index.shape[0], 8)
    ]
    return pieces[0] if len(pieces) == 1 else jnp.concatenate(pieces, axis=0)


def three_parts(x):
    high = x.astype(jnp.bfloat16).astype(jnp.float32)
    rest = x - high
    mid = rest.astype(jnp.bfloat16).astype(jnp.float32)
    return high, mid, rest - mid


def dot_nt(x, onehot):
    return lax.dot_general(
        x, onehot, (((1,), (1,)), ((), ())), preferred_element_type=jnp.float32
    )


def stacked_parts(x):
    high = x.astype(jnp.bfloat16)
    rest = x - high.astype(jnp.float32)
    mid = rest.astype(jnp.bfloat16)
    low = (rest - mid.astype(jnp.float32)).astype(jnp.bfloat16)
    return jnp.concatenate([high, mid, low], axis=0)


def add_parts(out):
    rows = out.shape[0] // 3
    return out[:rows] + (out[rows : 2 * rows] + out[2 * rows :])


def col_sum(x):
    return jnp.sum(x, axis=0, keepdims=True)


def lower_solve(f, a, b, c):
    one = a * f[0]
    two = (b - f[1] * one) * f[3]
    three = (c - f[2] * one - f[4] * two) * f[5]
    return one, two, three


def upper_solve(f, a, b, c):
    three = c * f[5]
    two = (b - f[4] * three) * f[3]
    one = (a - f[1] * two - f[2] * three) * f[0]
    return one, two, three


def normal_solve(f, a, b, c):
    return upper_solve(f, *lower_solve(f, a, b, c))


def cholesky_three(v):
    inv_first = 1.0 / jnp.sqrt(v[0])
    low_one = v[1] * inv_first
    low_two = v[2] * inv_first
    inv_second = 1.0 / jnp.sqrt(v[3] - low_one * low_one)
    low_three = (v[4] - low_two * low_one) * inv_second
    inv_third = 1.0 / jnp.sqrt(v[5] - low_two * low_two - low_three * low_three)
    return inv_first, low_one, low_two, inv_second, low_three, inv_third


def make_kernel(n_row, n_col, n_cl, n_obs):
    f32 = jnp.float32

    tiles_n = n_obs // LANES
    dense = tiles_n * n_cl

    def kernel(
        pairs_in, cj_in, lj_in, re_in, oc_in, ol_in, damp_in,
        cam_ref, land_ref,
        pairs_ref, cj_ref, lj_ref, re_ref, oc_ref, ol_ref, damp_ref, s0,
        one_cam, one_land, ustat, wstat, xstat, bstat, res, vecs, fac, yvec,
        msg1, msg2, in1, zbuf, in2, in3, in4, in5, qbuf, own, stot,
        s1, r1, s2, r2, s3, r3, s4, r4, s5, r5, s6, r6, s7, r7,
    ):
        one = jnp.asarray(1, jnp.bfloat16)
        nil = jnp.asarray(0, jnp.bfloat16)
        row = lax.axis_index("row")
        col = lax.axis_index("col")
        hub_col = row // 2
        is_hub = col == hub_col
        z, x = row // SIDE, lax.rem(row, SIDE)
        zs = [lax.rem(z + d, SIDE) * SIDE for d in range(SIDE)]
        xs = [lax.rem(x + d, SIDE) for d in range(SIDE)]
        cols = [lax.rem(col + d, n_col) for d in range(n_col)]
        up = lambda i: zs[i // SIDE] + xs[i % SIDE]
        over = lambda i: cols[i]

        def apart(i):
            return sum(min(d, SIDE - d) for d in (i // SIDE, i % SIDE))

        plane = sorted(range(1, n_row), key=lambda i: -apart(i))
        ring = [*range(2, n_col - 1), 1, n_col - 1]

        loads = [
            pltpu.make_async_copy(source, target, s0.at[n])
            for n, (source, target) in enumerate(
                (
                    (oc_in, oc_ref),
                    (ol_in, ol_ref),
                    (lj_in, lj_ref),
                    (re_in, re_ref),
                    (cj_in, cj_ref),
                    (pairs_in, pairs_ref),
                    (damp_in, damp_ref),
                )
            )
        ]
        for load in loads:
            load.start()

        barrier = pltpu.get_barrier_semaphore()

        @pl.when(is_hub)
        def _():
            for i in plane:
                pl.semaphore_signal(barrier, inc=1, device_id=(up(i), col), device_id_type=MESH)
            for i in range(1, n_col):
                pl.semaphore_signal(barrier, inc=1, device_id=(row, over(i)), device_id_type=MESH)

        def place(tiles, out, k):
            rolled = pltpu.roll(out, 64, axis=1)
            half = lax.broadcasted_iota(jnp.int32, out.shape, 1) < 64

            def pick(cond, x):
                return jnp.where(cond, x, 0.0)

            a, b = first[k], second[k]
            return (
                tiles[0] + jnp.where(half, pick(a == 0, out), pick(a == 1, rolled)),
                tiles[1] + jnp.where(half, pick(b == 0, rolled), pick(b == 1, out)),
                tiles[2] + jnp.where(half, pick(b == 2, rolled), pick(b == 3, out)),
            )

        def jac(r, a):
            return cj_ref[(r * 9 + a) * dense : (r * 9 + a + 1) * dense, :]

        def land_jac(r, b):
            return lj_ref[(r * 3 + b) * dense : (r * 3 + b + 1) * dense, :]

        def put(ref, q, value):
            ref[q * dense : (q + 1) * dense, :] = value

        def of_cluster(ref, k, rows):
            return jnp.concatenate(
                [ref[pl.ds(j * n_cl + k, rows, stride=dense), :] for j in range(tiles_n)], axis=1
            )

        def put_result(k, value):
            rows = value.shape[0]
            res[k * 32 : k * 32 + rows, :] = value
            res[(k + n_cl) * 32 : (k + n_cl) * 32 + rows, :] = value

        def result(q):
            return res[pl.ds(q, 2 * n_cl, stride=32), :]

        loads[0].wait()
        loads[1].wait()
        cams = oc_ref[...]
        lands = ol_ref[...]

        cams_f = cams.astype(f32)
        lands_f = lands.astype(f32)

        def packed_row(x, j, k):
            at = j * n_cl + k
            return jnp.broadcast_to(x[at : at + 1, :], (16, LANES)).astype(jnp.bfloat16)

        level = [
            (lax.broadcasted_iota(jnp.int32, (16, LANES), 0) + 16 * i).astype(f32).astype(jnp.bfloat16)
            for i in range(8)
        ]
        for k in range(n_cl):
            for j in range(tiles_n):
                land_row = packed_row(lands_f, j, k)
                cam_row = packed_row(cams_f, j, k)
                for i in range(8):
                    at = (k, slice(16 * i, 16 * i + 16), slice(j * LANES, (j + 1) * LANES))
                    one_land[at] = jnp.where(level[i] == land_row, one, nil)
                    one_cam[at] = jnp.where(level[i] == cam_row, one, nil)

        power = jnp.full((dense, LANES), 2.0**-64, f32)
        for i in range(7):
            power = power * jnp.where(((cams >> i) & 1) == 1, 2.0 ** (2**i), 1.0)
        code = power * (1.0 + lands_f * (1.0 / 128.0))
        code_t = code.T

        zero = jnp.zeros((dense, LANES), f32)
        for q in range(27, 32):
            put(xstat, q, zero)
            put(ustat, q, zero)
        for q in range(18, 24):
            put(wstat, q, zero)
        for q in range(9, 16):
            put(bstat, q, zero)
        loads[2].wait()
        loads[3].wait()
        ka = [land_jac(0, b) for b in range(3)]
        kb = [land_jac(1, b) for b in range(3)]
        e0, e1 = (
            jnp.concatenate(
                [re_ref[pl.ds(2 * j + r, n_cl, stride=2 * tiles_n), :] for j in range(tiles_n)], axis=0
            )
            for r in range(2)
        )
        stats = [
            ka[i] * ka[j] + kb[i] * kb[j]
            for i, j in ((0, 0), (0, 1), (0, 2), (1, 1), (1, 2), (2, 2))
        ] + [ka[b] * e0 + kb[b] * e1 for b in range(3)]
        for q, stat in enumerate(stats):
            for p, part in enumerate(three_parts(stat)):
                put(xstat, p * 9 + q, part)
        for k in range(n_cl):
            put_result(k, dot_nt(of_cluster(xstat, k, 32).astype(jnp.bfloat16), one_land[k]))
        v = [result(q) + (result(9 + q) + result(18 + q)) for q in range(9)]
        v[0], v[3], v[5] = v[0] + DAMPING, v[3] + DAMPING, v[5] + DAMPING
        factor = cholesky_three(v[:6])
        base = normal_solve(factor, v[6], v[7], v[8])
        for i in range(6):
            fac[i] = factor[i]
        for b in range(3):
            yvec[b] = base[b]

        loads[4].wait()
        loads[5].wait()
        loads[6].wait()
        first = [pairs_ref[0, k] - 2 * row for k in range(n_cl)]
        second = [pairs_ref[1, k] - 4 * col for k in range(n_cl)]

        lane = lax.broadcasted_iota(jnp.int32, (16, LANES), 1)
        sub = lax.broadcasted_iota(jnp.int32, (16, LANES), 0)
        flat = (lane - 16 * col) * 9 + sub
        mine = (lane >= 16 * col) & (lane < 16 * col + 16) & (sub < 9)
        flat = jnp.where(mine, flat, 0)
        damp_low = jnp.broadcast_to(damp_ref[:, :LANES], (8, LANES))
        damp_high = jnp.broadcast_to(
            jnp.concatenate([damp_ref[:, LANES:], jnp.zeros((1, 2 * LANES - 144), f32)], axis=1),
            (8, LANES),
        )
        damp = jnp.where(
            flat < LANES,
            lane_gather(damp_low, jnp.minimum(flat, LANES - 1)),
            lane_gather(damp_high, jnp.maximum(flat - LANES, 0)),
        )
        damp = jnp.where(mine, damp, 0.0)

        f = [lane_gather(factor[i], lands) for i in range(6)]
        g = [lane_gather(base[b], lands) for b in range(3)]
        w0 = ka[0] * g[0] + ka[1] * g[1] + ka[2] * g[2] - e0
        w1 = kb[0] * g[0] + kb[1] * g[1] + kb[2] * g[2] - e1
        for a in range(9):
            j0, j1 = jac(0, a), jac(1, a)
            solved = lower_solve(f, *[j0 * ka[b] + j1 * kb[b] for b in range(3)])
            for b in range(3):
                put(ustat, b * 8 + a if a < 8 else 24 + b, solved[b])
            put(wstat, a if a < 8 else 16, j0 * w0 + j1 * w1)
            put(wstat, 8 + a if a < 8 else 17, j0 * j0 + j1 * j1)
        zero = jnp.zeros((32, LANES), f32)
        tiles = (zero, zero, zero)
        for k in range(n_cl):
            rows_packed = [
                jnp.concatenate([packed_row(code, j, k)] * 8, axis=0) for j in range(tiles_n)
            ]
            blocks = []
            for j in range(tiles_n):
                at = j * n_cl + k
                column = jnp.broadcast_to(code_t[:, at : at + 1], (LANES, LANES)).astype(jnp.bfloat16)
                blocks.append(
                    jnp.concatenate([jnp.where(column == r, one, nil) for r in rows_packed], axis=1)
                )
            match = jnp.concatenate(blocks, axis=0)
            solved = of_cluster(ustat, k, 32)
            paired = add_parts(
                jnp.dot(stacked_parts(solved), match, preferred_element_type=jnp.float32)
            )
            square = solved * paired
            plain = of_cluster(wstat, k, 24)
            diag = plain[8:16] - (square[0:8] + square[8:16] + square[16:24])
            lhs = jnp.concatenate([plain[0:8], diag, plain[16:24], square[24:32]], axis=0)
            tiles = place(tiles, add_parts(dot_nt(stacked_parts(lhs), one_cam[k])), k)
        for i in range(3):
            extra = damp if i == 0 else jnp.zeros((16, LANES), f32)
            t = tiles[i]
            msg1[i, 0:8, :] = t[0:8]
            msg1[i, 8:16, :] = t[8:16] + extra[0:8]
            msg1[i, 16:17, :] = t[16:17]
            msg1[i, 17:18, :] = t[17:18] - (t[24:25] + t[25:26] + t[26:27]) + extra[8:9]

        pl.semaphore_wait(barrier, jnp.where(is_hub, 1, 3))

        def many(ref, send_sem, recv_sem):
            return pltpu.make_async_remote_copy(
                src_ref=ref,
                dst_ref=ref,
                send_sem=send_sem,
                recv_sem=recv_sem,
                device_id=(row, over(1)),
                device_id_type=MESH,
            )

        hub_of = ((row, hub_col), (2 * col, col), (2 * col + 1, col))

        def contribution(msg, buf, send, recv, i):
            row_slot = lax.rem(col - hub_col + n_col, n_col)
            hub_z, hub_x = (2 * col + i - 1) // SIDE, lax.rem(2 * col + i - 1, SIDE)
            plane_slot = lax.rem(z - hub_z + SIDE, SIDE) * SIDE + lax.rem(x - hub_x + SIDE, SIDE)
            slot = row_slot if i == 0 else n_col + plane_slot
            return pltpu.make_async_remote_copy(
                src_ref=msg.at[i],
                dst_ref=buf.at[slot],
                send_sem=send,
                recv_sem=recv.at[0 if i == 0 else 1],
                device_id=hub_of[i],
                device_id_type=MESH,
            )

        def not_self(i):
            return jnp.logical_not(is_hub) if i == 0 else row != 2 * col + (i - 1)

        def to_hubs(msg, buf, send, recv):
            for i in range(3):
                @pl.when(not_self(i))
                def _():
                    contribution(msg, buf, send, recv, i).start()

        def sent_to_hubs(msg, send, recv):
            @pl.when(is_hub)
            def _():
                many(msg.at[pl.ds(0, 1)], send, recv.at[0]).wait_send()

            @pl.when(jnp.logical_not(is_hub))
            def _():
                many(msg, send, recv.at[0]).wait_send()

        def at_hub(msg, buf, send, recv):
            mine_tile = 1 + row - 2 * col
            total = msg[0] + msg[mine_tile]
            late = [n_col + i for i in plane[::-1]]
            many(buf.at[pl.ds(1, n_col - 1)], send, recv.at[0]).wait_recv()
            many(buf.at[pl.ds(n_col + 1, n_row - 1)], send, recv.at[1]).wait_recv()
            for slot in [*ring, *late]:
                total = total + buf[slot]
            return total

        def spread_copy(buf, send, recv, j):
            mine_tile = 1 + row - 2 * col
            if j < n_col:
                target, slot = (row, over(j)), 0
            else:
                target, slot = (up(j - n_col), col), mine_tile
            return pltpu.make_async_remote_copy(
                src_ref=buf.at[0],
                dst_ref=buf.at[slot],
                send_sem=send,
                recv_sem=recv.at[slot],
                device_id=target,
                device_id_type=MESH,
            )

        others = [*[n_col + i for i in plane], *ring]

        def spread(buf, send, recv):
            for j in others:
                spread_copy(buf, send, recv, j).start()

        def spread_done(proxy, send, recv):
            @pl.when(is_hub)
            def _():
                many(proxy.at[pl.ds(0, n_row + n_col - 2)], send, recv.at[0]).wait_send()

        def arrived(buf, send, recv):
            for i in range(3):
                @pl.when(not_self(i))
                def _():
                    pltpu.make_async_remote_copy(
                        src_ref=buf.at[0],
                        dst_ref=buf.at[i],
                        send_sem=send,
                        recv_sem=recv.at[i],
                        device_id=(row, over(1)),
                        device_id_type=MESH,
                    ).wait_recv()

        left = lax.broadcasted_iota(jnp.int32, (9, LANES), 1) < 64

        def pushed(tiles):
            rolled = [pltpu.roll(t, 64, axis=1) for t in tiles]
            for k in range(n_cl):
                a, b = first[k], second[k]
                own = jnp.where(a == 0, tiles[0], rolled[0])
                odd = jnp.where(b < 2, tiles[1], tiles[2])
                even = jnp.where(b < 2, rolled[1], rolled[2])
                vec = jnp.where(left, own, jnp.where((b == 1) | (b == 3), odd, even))
                vecs[k * 16 : k * 16 + 9, :] = vec
                vecs[(k + n_cl) * 16 : (k + n_cl) * 16 + 9, :] = vec
            m0 = m1 = None
            for a in range(9):
                at_obs = lane_gather(vecs[pl.ds(a, 2 * n_cl, stride=16), :], cams)
                p0, p1 = jac(0, a) * at_obs, jac(1, a) * at_obs
                m0, m1 = (p0, p1) if m0 is None else (m0 + p0, m1 + p1)
            for b in range(3):
                back = land_jac(0, b) * m0 + land_jac(1, b) * m1
                for p, part in enumerate(three_parts(back)):
                    put(bstat, p * 3 + b, part)
            for k in range(n_cl):
                put_result(k, dot_nt(of_cluster(bstat, k, 16).astype(jnp.bfloat16), one_land[k]))
            total = [result(b) + (result(3 + b) + result(6 + b)) for b in range(3)]
            return m0, m1, total, normal_solve([fac[i] for i in range(6)], *total)

        to_hubs(msg1, in1, s1, r1)

        @pl.when(is_hub)
        def _():
            total = at_hub(msg1, in1, s1, r1)
            zbuf[0, 0:8, :] = total[0:8] / total[8:16]
            zbuf[0, 8:9, :] = total[16:17] / total[17:18]
            zbuf[0, 9:17, :] = total[8:16]
            zbuf[0, 17:18, :] = total[17:18]
            spread(zbuf, s2, r2)
            zbuf[1 + row - 2 * col] = zbuf[0]

        arrived(zbuf, s2, r2)

        z_tiles = tuple(zbuf[i, 0:9, :] for i in range(3))
        m0, m1, b, y = pushed(z_tiles)
        for i in range(3):
            yvec[3 + i] = y[i]
        w0, w1 = m0, m1
        for i in range(3):
            g = lane_gather(y[i], lands)
            w0 = w0 - land_jac(0, i) * g
            w1 = w1 - land_jac(1, i) * g
        for a in range(9):
            for p, part in enumerate(three_parts(jac(0, a) * w0 + jac(1, a) * w1)):
                put(xstat, p * 8 + a if a < 8 else 24 + p, part)
        zero = jnp.zeros((16, LANES), f32)
        tiles = (zero, zero, zero)
        for k in range(n_cl):
            out = dot_nt(of_cluster(xstat, k, 32).astype(jnp.bfloat16), one_cam[k])
            out = jnp.concatenate([out[0:8] + (out[8:16] + out[16:24]), out[24:32]], axis=0)
            tiles = place(tiles, out, k)
        for i in range(3):
            t = tiles[i]
            low, high = t[0:8], t[8:9] + (t[9:10] + t[10:11])
            if i == 0:
                low = low + damp[0:8] * z_tiles[0][0:8]
                high = high + damp[8:9] * z_tiles[0][8:9]
            msg2[i, 0:8, :] = low
            msg2[i, 8:9, :] = high
        parity = lax.rem(row, 2)

        def send(source, target_ref, send_sem, recv_sem, device):
            return pltpu.make_async_remote_copy(
                src_ref=source,
                dst_ref=target_ref,
                send_sem=send_sem,
                recv_sem=recv_sem,
                device_id=device,
                device_id_type=MESH,
            )

        def ring_copy(i):
            return send(msg2.at[0], in2.at[i], s3, r3, (row, over(i)))

        def plane_copy(i):
            return send(msg2.at[pl.ds(1, 2)], in3.at[i], s4, r4, (up(i), col))

        def row_copy(i):
            slot = parity * n_col + col
            return send(msg2.at[0], in4.at[slot], s6, r6.at[parity], (up(i), hub_col))

        def col_copy(j, i):
            return send(msg2.at[1 + j], in5.at[row], s7, r7, (2 * col + j, over(i)))

        sends = [
            *[row_copy(i) for i in plane if apart(i) > 2],
            *[col_copy(j, i) for i in ring[:-2] for j in range(2)],
            *[row_copy(i) for i in plane if apart(i) <= 2],
            *[col_copy(j, i) for i in ring[-2:] for j in range(2)],
            *[plane_copy(i) for i in plane],
            *[ring_copy(i) for i in ring],
        ]
        for copy in sends:
            copy.start()

        many(in2.at[pl.ds(1, n_col - 1)], s3, r3).wait_recv()
        q_row = msg2[0]
        for i in ring:
            q_row = q_row + in2[i]
        many(in3.at[pl.ds(1, n_row - 1)], s4, r4).wait_recv()
        q_col = [msg2[1], msg2[2]]
        for i in plane[::-1]:
            q_col = [q_col[j] + in3[i, j] for j in range(2)]

        @pl.when(jnp.logical_not(is_hub))
        def _():
            many(in5, s7, r7).wait_recv()
            total = in5[0]
            for i in range(1, n_row):
                total = total + in5[i]
            qbuf[0] = total

        @pl.when(is_hub)
        def _():
            qbuf[0] = jnp.where(row == 2 * col, q_col[0], q_col[1])

        for j in range(2):
            @pl.when(row != 2 * col + j)
            def _():
                many(in4.at[pl.ds(j * n_col, n_col)], s6, r6.at[j]).wait_recv()
                total = in4[j * n_col]
                for i in range(1, n_col):
                    total = total + in4[j * n_col + i]
                qbuf[1 + j] = total

            @pl.when(row == 2 * col + j)
            def _():
                qbuf[1 + j] = q_row

        q_tiles = (q_row + qbuf[0], q_col[0] + qbuf[1], q_col[1] + qbuf[2])
        t_tiles = tuple(q_tiles[i] / zbuf[i, 9:18, :] - z_tiles[i] for i in range(3))
        at_hub_only = jnp.where(is_hub, zbuf[0, 9:18, :], 0.0)
        own[0:1, :] = col_sum(at_hub_only * z_tiles[0] * z_tiles[0])
        own[1:2, :] = col_sum(at_hub_only * z_tiles[0] * t_tiles[0])
        own[2:3, :] = col_sum(at_hub_only * t_tiles[0] * t_tiles[0])

        m0, m1, b, y = pushed(t_tiles)
        for i in range(3):
            yvec[6 + i] = y[i]
        square = m0 * m0 + m1 * m1
        form = -0.5 * (b[0] * y[0] + b[1] * y[1] + b[2] * y[2])
        for at in range(0, dense, 8):
            form = form + square[at : at + 8]
        t = t_tiles[0]
        form = form + damp[0:8] * t[0:8] * t[0:8]
        own[3:4, :] = col_sum(form) + damp[8:9] * t[8:9] * t[8:9]

        quarter = lax.broadcasted_iota(jnp.int32, (4, LANES), 1) // 32
        which = lax.broadcasted_iota(jnp.int32, (4, LANES), 0)
        four = own[...]
        four = four + pltpu.roll(four, 64, axis=1)
        four = four + pltpu.roll(four, 32, axis=1)
        stot[0:1, :] = col_sum(jnp.where(quarter == which, four, 0.0))

        def total_copy(i, j):
            slot = i * n_col + j
            return pltpu.make_async_remote_copy(
                src_ref=stot.at[pl.ds(0, 1)],
                dst_ref=stot.at[pl.ds(slot, 1)],
                send_sem=s5,
                recv_sem=r5,
                device_id=(up(i), over(j)),
                device_id_type=MESH,
            )

        def total_wait():
            return pltpu.make_async_remote_copy(
                src_ref=stot.at[pl.ds(1, n_row * n_col - 1)],
                dst_ref=stot.at[pl.ds(1, n_row * n_col - 1)],
                send_sem=s5,
                recv_sem=r5,
                device_id=(row, over(1)),
                device_id_type=MESH,
            )

        far = sorted(
            [(i, j) for i in range(n_row) for j in range(n_col) if i or j],
            key=lambda ij: -(apart(ij[0]) + min(ij[1], n_col - ij[1]) / 2),
        )
        for i, j in far:
            total_copy(i, j).start()

        def chosen(tile, first_entry, count):
            entry = lax.broadcasted_iota(jnp.int32, (8, LANES), 1) + first_entry
            level = lax.broadcasted_iota(jnp.int32, (8, LANES), 0)
            entry = jnp.minimum(entry, 143)
            cam = entry // 9
            rest = entry - 9 * cam
            at = cam + 16 * col
            low = jnp.where(rest == level, lane_gather(tile[0:8], at), 0.0)
            high = lane_gather(jnp.broadcast_to(tile[8:9], (8, LANES)), at)
            return col_sum(low + jnp.where((rest == 8) & (level == 0), high, 0.0))[:, :count]

        z_own = jnp.concatenate([chosen(z_tiles[0], 0, 128), chosen(z_tiles[0], 128, 16)], axis=1)
        t_own = jnp.concatenate([chosen(t_tiles[0], 0, 128), chosen(t_tiles[0], 128, 16)], axis=1)

        sent_to_hubs(msg1, s1, r1)
        spread_done(in1, s2, r2)

        many(in2.at[pl.ds(1, n_col - 1)], s3, r3).wait_send()
        many(in3.at[pl.ds(1, n_row - 1)], s4, r4).wait_send()
        many(in5.at[pl.ds(1, n_row - 1)], s6, r7).wait_send()
        many(in4.at[pl.ds(2, 2 * n_col - 2)], s7, r7).wait_send()

        total_wait().wait_recv()
        total = jnp.where(quarter == which, col_sum(stot[...]), 0.0)
        scalars = jnp.sum(total, axis=1, keepdims=True)
        rz, e, f, h = (scalars[i : i + 1] for i in range(4))
        pq = rz + e
        a0 = rz / pq
        new = a0 * ((rz * f - e * e) / pq)
        g = e / pq + new / rz
        curve = g * g * pq - 2.0 * g * a0 * (e + f) + a0 * a0 * h
        a1 = new / curve
        big_a = a0 + a1 * g
        big_b = -a1 * a0
        cam_ref[...] = big_a * z_own + big_b * t_own
        for b in range(3):
            land = -(yvec[b] + big_a * yvec[3 + b] + big_b * yvec[6 + b])
            land_ref[b] = land[0:n_cl]
        total_wait().wait_send()

    return kernel


def write_out(cam_ref, land_ref, cam_out, land_out, sem):
    copies = (
        pltpu.make_async_copy(cam_ref, cam_out, sem.at[0]),
        pltpu.make_async_copy(land_ref, land_out, sem.at[1]),
    )
    for copy in copies:
        copy.start()
    for copy in copies:
        copy.wait()


def per_device(cam_jac, land_jac, resid, obs_cam, obs_land, pairs, cam_damp):
    n_row = lax.axis_size("row")
    n_col = lax.axis_size("col")
    n_cl, _, n_obs = cam_jac.shape
    shard = cam_damp.shape[0]
    f32 = jnp.float32
    slots = n_row + n_col
    tiles = n_obs // LANES
    dense = n_cl * tiles
    vmem = pl.BlockSpec(memory_space=pltpu.VMEM)
    dma = pltpu.SemaphoreType.DMA

    def entries_first(x):
        return (
            x.reshape(n_cl, -1, tiles, LANES).transpose(1, 2, 0, 3).reshape(-1, LANES)
        )

    cam, land = pl.pallas_call(
        make_kernel(n_row, n_col, n_cl, n_obs),
        out_shape=(
            jax.ShapeDtypeStruct((1, shard), f32),
            jax.ShapeDtypeStruct((3, n_cl, LANES), f32),
        ),
        in_specs=[pl.BlockSpec(memory_space=pltpu.HBM)] * 7,
        out_specs=(vmem, vmem),
        scratch_shapes=[
            pltpu.SMEM((2, n_cl), jnp.int32),
            pltpu.VMEM((18 * dense, LANES), f32),
            pltpu.VMEM((6 * dense, LANES), f32),
            pltpu.VMEM((2 * dense, LANES), f32),
            pltpu.VMEM((dense, LANES), jnp.int32),
            pltpu.VMEM((dense, LANES), jnp.int32),
            pltpu.VMEM((1, shard), f32),
            dma((7,)),
            pltpu.VMEM((n_cl, LANES, n_obs), jnp.bfloat16),
            pltpu.VMEM((n_cl, LANES, n_obs), jnp.bfloat16),
            pltpu.VMEM((32 * dense, LANES), f32),
            pltpu.VMEM((24 * dense, LANES), f32),
            pltpu.VMEM((32 * dense, LANES), f32),
            pltpu.VMEM((16 * dense, LANES), f32),
            pltpu.VMEM((2 * n_cl * 32, LANES), f32),
            pltpu.VMEM((2 * n_cl * 16, LANES), f32),
            pltpu.VMEM((6, 8, LANES), f32),
            pltpu.VMEM((9, 8, LANES), f32),
            pltpu.VMEM((3, 18, LANES), f32),
            pltpu.VMEM((3, 9, LANES), f32),
            pltpu.VMEM((slots, 18, LANES), f32),
            pltpu.VMEM((3, 18, LANES), f32),
            pltpu.VMEM((n_col, 9, LANES), f32),
            pltpu.VMEM((n_row, 2, 9, LANES), f32),
            pltpu.VMEM((2 * n_col, 9, LANES), f32),
            pltpu.VMEM((n_row, 9, LANES), f32),
            pltpu.VMEM((3, 9, LANES), f32),
            pltpu.VMEM((4, LANES), f32),
            pltpu.VMEM((n_row * n_col, LANES), f32),
            dma, dma((2,)),
            dma, dma((3,)),
            dma, dma,
            dma, dma,
            dma, dma,
            dma, dma((2,)),
            dma, dma,
        ],
        compiler_params=pltpu.CompilerParams(collective_id=0, has_side_effects=True, vmem_limit_bytes=VMEM),
        name="schur_step",
    )(
        *(
            pltpu.with_memory_space_constraint(x, pltpu.HBM)
            for x in (
        pairs.T,
        entries_first(cam_jac),
        entries_first(land_jac),
        resid.reshape(n_cl, 2, tiles, LANES).transpose(0, 2, 1, 3).reshape(-1, LANES),
        obs_cam.reshape(n_cl, tiles, LANES).transpose(1, 0, 2).reshape(-1, LANES),
        obs_land.reshape(n_cl, tiles, LANES).transpose(1, 0, 2).reshape(-1, LANES),
        cam_damp.reshape(1, shard),
            )
        )
    )
    cam, land = pl.pallas_call(
        write_out,
        out_shape=(
            jax.ShapeDtypeStruct((1, shard), f32),
            jax.ShapeDtypeStruct((3, n_cl, LANES), f32),
        ),
        in_specs=[vmem] * 2,
        out_specs=[pl.BlockSpec(memory_space=pltpu.HBM)] * 2,
        scratch_shapes=[dma((2,))],
        compiler_params=pltpu.CompilerParams(vmem_limit_bytes=1 << 20),
        name="write_out",
    )(cam, land)
    return cam.reshape(shard), land.transpose(1, 0, 2)


def solution(mesh):
    in_specs = (
        P(("row", "col"), None, None),
        P(("row", "col"), None, None),
        P(("row", "col"), None, None),
        P(("row", "col"), None),
        P(("row", "col"), None),
        P(("row", "col"), None),
        P(("row", "col")),
    )
    out_specs = (P(("row", "col")), P(("row", "col"), None, None))
    return jax.shard_map(
        per_device, mesh=mesh, in_specs=in_specs, out_specs=out_specs, check_vma=False
    )
```

```python
import jax
import jax.numpy as jnp
from jax import lax
from jax.experimental import pallas as pl
from jax.experimental.pallas import tpu as pltpu
from jax.sharding import PartitionSpec as P

DAMPING = 1.0
MESH = pl.DeviceIdType.MESH
LANES = 128
SIDE = 4
VMEM = 8 << 20


def lane_gather(table, index):
    dims = lax.GatherDimensionNumbers((), (1,), (1,), (0,), (0,))
    pieces = [
        lax.gather(
            table,
            index[at : at + 8, :, None],
            dims,
            slice_sizes=(1, 1),
            mode=lax.GatherScatterMode.PROMISE_IN_BOUNDS,
        )
        for at in range(0, index.shape[0], 8)
    ]
    return pieces[0] if len(pieces) == 1 else jnp.concatenate(pieces, axis=0)


def three_parts(x):
    high = x.astype(jnp.bfloat16).astype(jnp.float32)
    rest = x - high
    mid = rest.astype(jnp.bfloat16).astype(jnp.float32)
    return high, mid, rest - mid


def dot_nt(x, onehot):
    return lax.dot_general(
        x, onehot, (((1,), (1,)), ((), ())), preferred_element_type=jnp.float32
    )


def stacked_parts(x):
    high = x.astype(jnp.bfloat16)
    rest = x - high.astype(jnp.float32)
    mid = rest.astype(jnp.bfloat16)
    low = (rest - mid.astype(jnp.float32)).astype(jnp.bfloat16)
    return jnp.concatenate([high, mid, low], axis=0)


def add_parts(out):
    rows = out.shape[0] // 3
    return out[:rows] + (out[rows : 2 * rows] + out[2 * rows :])


def col_sum(x):
    return jnp.sum(x, axis=0, keepdims=True)


def lower_solve(f, a, b, c):
    one = a * f[0]
    two = (b - f[1] * one) * f[3]
    three = (c - f[2] * one - f[4] * two) * f[5]
    return one, two, three


def upper_solve(f, a, b, c):
    three = c * f[5]
    two = (b - f[4] * three) * f[3]
    one = (a - f[1] * two - f[2] * three) * f[0]
    return one, two, three


def normal_solve(f, a, b, c):
    return upper_solve(f, *lower_solve(f, a, b, c))


def cholesky_three(v):
    inv_first = lax.rsqrt(v[0])
    low_one = v[1] * inv_first
    low_two = v[2] * inv_first
    inv_second = lax.rsqrt(v[3] - low_one * low_one)
    low_three = (v[4] - low_two * low_one) * inv_second
    inv_third = lax.rsqrt(v[5] - low_two * low_two - low_three * low_three)
    return inv_first, low_one, low_two, inv_second, low_three, inv_third


def make_kernel(n_row, n_col, n_cl, n_obs):
    f32 = jnp.float32

    tiles_n = n_obs // LANES
    dense = tiles_n * n_cl

    def kernel(
        pairs_in, cj_in, lj_in, re_in, oc_in, ol_in, damp_in,
        cam_ref, land_ref,
        pairs_ref, cj_ref, lj_ref, re_ref, oc_ref, ol_ref, damp_ref, s0,
        one_cam, one_land, ustat, wstat, xstat, bstat, res, vecs, fac, yvec,
        msg1, msg2, in1, zbuf, in2, in3, in4, in5, qbuf, own, stot,
        s1, r1, s2, r2, s3, r3, s4, r4, s5, r5, s6, r6, s7, r7,
    ):
        one = jnp.asarray(1, jnp.bfloat16)
        nil = jnp.asarray(0, jnp.bfloat16)
        row = lax.axis_index("row")
        col = lax.axis_index("col")
        hub_col = row // 2
        is_hub = col == hub_col
        z, x = row // SIDE, lax.rem(row, SIDE)
        zs = [lax.rem(z + d, SIDE) * SIDE for d in range(SIDE)]
        xs = [lax.rem(x + d, SIDE) for d in range(SIDE)]
        cols = [lax.rem(col + d, n_col) for d in range(n_col)]
        up = lambda i: zs[i // SIDE] + xs[i % SIDE]
        over = lambda i: cols[i]

        def apart(i):
            return sum(min(d, SIDE - d) for d in (i // SIDE, i % SIDE))

        plane = sorted(range(1, n_row), key=lambda i: -apart(i))
        ring = [*range(2, n_col - 1), 1, n_col - 1]

        loads = [
            pltpu.make_async_copy(source, target, s0.at[n])
            for n, (source, target) in enumerate(
                (
                    (oc_in, oc_ref),
                    (ol_in, ol_ref),
                    (lj_in, lj_ref),
                    (re_in, re_ref),
                    (cj_in, cj_ref),
                    (pairs_in, pairs_ref),
                    (damp_in, damp_ref),
                )
            )
        ]
        for load in loads:
            load.start()

        barrier = pltpu.get_barrier_semaphore()

        @pl.when(is_hub)
        def _():
            for i in plane:
                pl.semaphore_signal(barrier, inc=1, device_id=(up(i), col), device_id_type=MESH)
            for i in range(1, n_col):
                pl.semaphore_signal(barrier, inc=1, device_id=(row, over(i)), device_id_type=MESH)

        def place(tiles, out, k):
            rolled = pltpu.roll(out, 64, axis=1)
            half = lax.broadcasted_iota(jnp.int32, out.shape, 1) < 64

            def pick(cond, x):
                return jnp.where(cond, x, 0.0)

            a, b = first[k], second[k]
            return (
                tiles[0] + jnp.where(half, pick(a == 0, out), pick(a == 1, rolled)),
                tiles[1] + jnp.where(half, pick(b == 0, rolled), pick(b == 1, out)),
                tiles[2] + jnp.where(half, pick(b == 2, rolled), pick(b == 3, out)),
            )

        def jac(r, a):
            return cj_ref[(r * 9 + a) * dense : (r * 9 + a + 1) * dense, :]

        def land_jac(r, b):
            return lj_ref[(r * 3 + b) * dense : (r * 3 + b + 1) * dense, :]

        def put(ref, q, value):
            ref[q * dense : (q + 1) * dense, :] = value

        def of_cluster(ref, k, rows):
            return jnp.concatenate(
                [ref[pl.ds(j * n_cl + k, rows, stride=dense), :] for j in range(tiles_n)], axis=1
            )

        def put_result(k, value):
            rows = value.shape[0]
            res[k * 32 : k * 32 + rows, :] = value
            res[(k + n_cl) * 32 : (k + n_cl) * 32 + rows, :] = value

        def result(q):
            return res[pl.ds(q, 2 * n_cl, stride=32), :]

        loads[0].wait()
        loads[1].wait()
        cams = oc_ref[...]
        lands = ol_ref[...]

        cams_f = cams.astype(f32)
        lands_f = lands.astype(f32)

        def packed_row(x, j, k):
            at = j * n_cl + k
            return jnp.broadcast_to(x[at : at + 1, :], (16, LANES)).astype(jnp.bfloat16)

        level = [
            (lax.broadcasted_iota(jnp.int32, (16, LANES), 0) + 16 * i).astype(f32).astype(jnp.bfloat16)
            for i in range(8)
        ]
        for k in range(n_cl):
            for j in range(tiles_n):
                land_row = packed_row(lands_f, j, k)
                cam_row = packed_row(cams_f, j, k)
                for i in range(8):
                    at = (k, slice(16 * i, 16 * i + 16), slice(j * LANES, (j + 1) * LANES))
                    one_land[at] = jnp.where(level[i] == land_row, one, nil)
                    one_cam[at] = jnp.where(level[i] == cam_row, one, nil)

        power = jnp.full((dense, LANES), 2.0**-64, f32)
        for i in range(7):
            power = power * jnp.where(((cams >> i) & 1) == 1, 2.0 ** (2**i), 1.0)
        code = power * (1.0 + lands_f * (1.0 / 128.0))
        code_t = code.T

        zero = jnp.zeros((dense, LANES), f32)
        for q in range(27, 32):
            put(xstat, q, zero)
            put(ustat, q, zero)
        for q in range(18, 24):
            put(wstat, q, zero)
        for q in range(9, 16):
            put(bstat, q, zero)
        loads[2].wait()
        loads[3].wait()
        ka = [land_jac(0, b) for b in range(3)]
        kb = [land_jac(1, b) for b in range(3)]
        e0, e1 = (
            jnp.concatenate(
                [re_ref[pl.ds(2 * j + r, n_cl, stride=2 * tiles_n), :] for j in range(tiles_n)], axis=0
            )
            for r in range(2)
        )
        stats = [
            ka[i] * ka[j] + kb[i] * kb[j]
            for i, j in ((0, 0), (0, 1), (0, 2), (1, 1), (1, 2), (2, 2))
        ] + [ka[b] * e0 + kb[b] * e1 for b in range(3)]
        for q, stat in enumerate(stats):
            for p, part in enumerate(three_parts(stat)):
                put(xstat, p * 9 + q, part)
        for k in range(n_cl):
            put_result(k, dot_nt(of_cluster(xstat, k, 32).astype(jnp.bfloat16), one_land[k]))
        v = [result(q) + (result(9 + q) + result(18 + q)) for q in range(9)]
        v[0], v[3], v[5] = v[0] + DAMPING, v[3] + DAMPING, v[5] + DAMPING
        factor = cholesky_three(v[:6])
        base = normal_solve(factor, v[6], v[7], v[8])
        for i in range(6):
            fac[i] = factor[i]
        for b in range(3):
            yvec[b] = base[b]

        loads[4].wait()
        loads[5].wait()
        loads[6].wait()
        first = [pairs_ref[0, k] - 2 * row for k in range(n_cl)]
        second = [pairs_ref[1, k] - 4 * col for k in range(n_cl)]

        lane = lax.broadcasted_iota(jnp.int32, (16, LANES), 1)
        sub = lax.broadcasted_iota(jnp.int32, (16, LANES), 0)
        flat = (lane - 16 * col) * 9 + sub
        mine = (lane >= 16 * col) & (lane < 16 * col + 16) & (sub < 9)
        flat = jnp.where(mine, flat, 0)
        damp_low = jnp.broadcast_to(damp_ref[:, :LANES], (8, LANES))
        damp_high = jnp.broadcast_to(
            jnp.concatenate([damp_ref[:, LANES:], jnp.zeros((1, 2 * LANES - 144), f32)], axis=1),
            (8, LANES),
        )
        damp = jnp.where(
            flat < LANES,
            lane_gather(damp_low, jnp.minimum(flat, LANES - 1)),
            lane_gather(damp_high, jnp.maximum(flat - LANES, 0)),
        )
        damp = jnp.where(mine, damp, 0.0)

        f = [lane_gather(factor[i], lands) for i in range(6)]
        g = [lane_gather(base[b], lands) for b in range(3)]
        w0 = ka[0] * g[0] + ka[1] * g[1] + ka[2] * g[2] - e0
        w1 = kb[0] * g[0] + kb[1] * g[1] + kb[2] * g[2] - e1
        for a in range(9):
            j0, j1 = jac(0, a), jac(1, a)
            solved = lower_solve(f, *[j0 * ka[b] + j1 * kb[b] for b in range(3)])
            for b in range(3):
                put(ustat, b * 8 + a if a < 8 else 24 + b, solved[b])
            put(wstat, a if a < 8 else 16, j0 * w0 + j1 * w1)
            put(wstat, 8 + a if a < 8 else 17, j0 * j0 + j1 * j1)
        zero = jnp.zeros((32, LANES), f32)
        tiles = (zero, zero, zero)
        for k in range(n_cl):
            rows_packed = [
                jnp.concatenate([packed_row(code, j, k)] * 8, axis=0) for j in range(tiles_n)
            ]
            blocks = []
            for j in range(tiles_n):
                at = j * n_cl + k
                column = jnp.broadcast_to(code_t[:, at : at + 1], (LANES, LANES)).astype(jnp.bfloat16)
                blocks.append(
                    jnp.concatenate([jnp.where(column == r, one, nil) for r in rows_packed], axis=1)
                )
            match = jnp.concatenate(blocks, axis=0)
            solved = of_cluster(ustat, k, 32)
            paired = add_parts(
                jnp.dot(stacked_parts(solved), match, preferred_element_type=jnp.float32)
            )
            square = solved * paired
            plain = of_cluster(wstat, k, 24)
            diag = plain[8:16] - (square[0:8] + square[8:16] + square[16:24])
            lhs = jnp.concatenate([plain[0:8], diag, plain[16:24], square[24:32]], axis=0)
            tiles = place(tiles, add_parts(dot_nt(stacked_parts(lhs), one_cam[k])), k)
        for i in range(3):
            extra = damp if i == 0 else jnp.zeros((16, LANES), f32)
            t = tiles[i]
            msg1[i, 0:8, :] = t[0:8]
            msg1[i, 8:16, :] = t[8:16] + extra[0:8]
            msg1[i, 16:17, :] = t[16:17]
            msg1[i, 17:18, :] = t[17:18] - (t[24:25] + t[25:26] + t[26:27]) + extra[8:9]

        pl.semaphore_wait(barrier, jnp.where(is_hub, 1, 3))

        def many(ref, send_sem, recv_sem):
            return pltpu.make_async_remote_copy(
                src_ref=ref,
                dst_ref=ref,
                send_sem=send_sem,
                recv_sem=recv_sem,
                device_id=(row, over(1)),
                device_id_type=MESH,
            )

        hub_of = ((row, hub_col), (2 * col, col), (2 * col + 1, col))

        def contribution(msg, buf, send, recv, i):
            row_slot = lax.rem(col - hub_col + n_col, n_col)
            hub_z, hub_x = (2 * col + i - 1) // SIDE, lax.rem(2 * col + i - 1, SIDE)
            plane_slot = lax.rem(z - hub_z + SIDE, SIDE) * SIDE + lax.rem(x - hub_x + SIDE, SIDE)
            slot = row_slot if i == 0 else n_col + plane_slot
            return pltpu.make_async_remote_copy(
                src_ref=msg.at[i],
                dst_ref=buf.at[slot],
                send_sem=send,
                recv_sem=recv.at[0 if i == 0 else 1],
                device_id=hub_of[i],
                device_id_type=MESH,
            )

        def not_self(i):
            return jnp.logical_not(is_hub) if i == 0 else row != 2 * col + (i - 1)

        def to_hubs(msg, buf, send, recv):
            for i in range(3):
                @pl.when(not_self(i))
                def _():
                    contribution(msg, buf, send, recv, i).start()

        def sent_to_hubs(msg, send, recv):
            @pl.when(is_hub)
            def _():
                many(msg.at[pl.ds(0, 1)], send, recv.at[0]).wait_send()

            @pl.when(jnp.logical_not(is_hub))
            def _():
                many(msg, send, recv.at[0]).wait_send()

        def at_hub(msg, buf, send, recv):
            mine_tile = 1 + row - 2 * col
            total = msg[0] + msg[mine_tile]
            late = [n_col + i for i in plane[::-1]]
            many(buf.at[pl.ds(1, n_col - 1)], send, recv.at[0]).wait_recv()
            many(buf.at[pl.ds(n_col + 1, n_row - 1)], send, recv.at[1]).wait_recv()
            slots = [*ring, *late]
            parts = [total, buf[slots[0]], buf[slots[1]], buf[slots[2]]]
            for n, slot in enumerate(slots[3:]):
                parts[n % 4] = parts[n % 4] + buf[slot]
            return (parts[0] + parts[1]) + (parts[2] + parts[3])

        def spread_copy(buf, send, recv, j):
            mine_tile = 1 + row - 2 * col
            if j < n_col:
                target, slot = (row, over(j)), 0
            else:
                target, slot = (up(j - n_col), col), mine_tile
            return pltpu.make_async_remote_copy(
                src_ref=buf.at[0],
                dst_ref=buf.at[slot],
                send_sem=send,
                recv_sem=recv.at[slot],
                device_id=target,
                device_id_type=MESH,
            )

        others = [*[n_col + i for i in plane], *ring]

        def spread(buf, send, recv):
            for j in others:
                spread_copy(buf, send, recv, j).start()

        def spread_done(proxy, send, recv):
            @pl.when(is_hub)
            def _():
                many(proxy.at[pl.ds(0, n_row + n_col - 2)], send, recv.at[0]).wait_send()

        def arrived(buf, send, recv):
            for i in range(3):
                @pl.when(not_self(i))
                def _():
                    pltpu.make_async_remote_copy(
                        src_ref=buf.at[0],
                        dst_ref=buf.at[i],
                        send_sem=send,
                        recv_sem=recv.at[i],
                        device_id=(row, over(1)),
                        device_id_type=MESH,
                    ).wait_recv()

        left = lax.broadcasted_iota(jnp.int32, (9, LANES), 1) < 64

        def pushed(tiles):
            rolled = [pltpu.roll(t, 64, axis=1) for t in tiles]
            for k in range(n_cl):
                a, b = first[k], second[k]
                own = jnp.where(a == 0, tiles[0], rolled[0])
                odd = jnp.where(b < 2, tiles[1], tiles[2])
                even = jnp.where(b < 2, rolled[1], rolled[2])
                vec = jnp.where(left, own, jnp.where((b == 1) | (b == 3), odd, even))
                vecs[k * 16 : k * 16 + 9, :] = vec
                vecs[(k + n_cl) * 16 : (k + n_cl) * 16 + 9, :] = vec
            m0 = m1 = None
            for a in range(9):
                at_obs = lane_gather(vecs[pl.ds(a, 2 * n_cl, stride=16), :], cams)
                p0, p1 = jac(0, a) * at_obs, jac(1, a) * at_obs
                m0, m1 = (p0, p1) if m0 is None else (m0 + p0, m1 + p1)
            for b in range(3):
                back = land_jac(0, b) * m0 + land_jac(1, b) * m1
                for p, part in enumerate(three_parts(back)):
                    put(bstat, p * 3 + b, part)
            for k in range(n_cl):
                put_result(k, dot_nt(of_cluster(bstat, k, 16).astype(jnp.bfloat16), one_land[k]))
            total = [result(b) + (result(3 + b) + result(6 + b)) for b in range(3)]
            return m0, m1, total, normal_solve([fac[i] for i in range(6)], *total)

        to_hubs(msg1, in1, s1, r1)

        @pl.when(is_hub)
        def _():
            total = at_hub(msg1, in1, s1, r1)
            zbuf[0, 0:8, :] = total[0:8] / total[8:16]
            zbuf[0, 8:9, :] = total[16:17] / total[17:18]
            zbuf[0, 9:17, :] = total[8:16]
            zbuf[0, 17:18, :] = total[17:18]
            spread(zbuf, s2, r2)
            zbuf[1 + row - 2 * col] = zbuf[0]

        arrived(zbuf, s2, r2)

        z_tiles = tuple(zbuf[i, 0:9, :] for i in range(3))
        m0, m1, b, y = pushed(z_tiles)
        for i in range(3):
            yvec[3 + i] = y[i]
        w0, w1 = m0, m1
        for i in range(3):
            g = lane_gather(y[i], lands)
            w0 = w0 - land_jac(0, i) * g
            w1 = w1 - land_jac(1, i) * g
        for a in range(9):
            for p, part in enumerate(three_parts(jac(0, a) * w0 + jac(1, a) * w1)):
                put(xstat, p * 8 + a if a < 8 else 24 + p, part)
        zero = jnp.zeros((16, LANES), f32)
        tiles = (zero, zero, zero)
        for k in range(n_cl):
            out = dot_nt(of_cluster(xstat, k, 32).astype(jnp.bfloat16), one_cam[k])
            out = jnp.concatenate([out[0:8] + (out[8:16] + out[16:24]), out[24:32]], axis=0)
            tiles = place(tiles, out, k)
        for i in range(3):
            t = tiles[i]
            low, high = t[0:8], t[8:9] + (t[9:10] + t[10:11])
            if i == 0:
                low = low + damp[0:8] * z_tiles[0][0:8]
                high = high + damp[8:9] * z_tiles[0][8:9]
            msg2[i, 0:8, :] = low
            msg2[i, 8:9, :] = high
        parity = lax.rem(row, 2)

        def send(source, target_ref, send_sem, recv_sem, device):
            return pltpu.make_async_remote_copy(
                src_ref=source,
                dst_ref=target_ref,
                send_sem=send_sem,
                recv_sem=recv_sem,
                device_id=device,
                device_id_type=MESH,
            )

        def ring_copy(i):
            return send(msg2.at[0], in2.at[i], s3, r3, (row, over(i)))

        def plane_copy(i):
            return send(msg2.at[pl.ds(1, 2)], in3.at[i], s4, r4, (up(i), col))

        def row_copy(i):
            slot = parity * n_col + col
            return send(msg2.at[0], in4.at[slot], s6, r6.at[parity], (up(i), hub_col))

        def col_copy(j, i):
            return send(msg2.at[1 + j], in5.at[row], s7, r7, (2 * col + j, over(i)))

        sends = [
            *[row_copy(i) for i in plane if apart(i) > 2],
            *[col_copy(j, i) for i in ring[:-2] for j in range(2)],
            *[row_copy(i) for i in plane if apart(i) <= 2],
            *[col_copy(j, i) for i in ring[-2:] for j in range(2)],
            *[plane_copy(i) for i in plane],
            *[ring_copy(i) for i in ring],
        ]
        for copy in sends:
            copy.start()

        many(in2.at[pl.ds(1, n_col - 1)], s3, r3).wait_recv()
        q_row = msg2[0]
        for i in ring:
            q_row = q_row + in2[i]
        many(in3.at[pl.ds(1, n_row - 1)], s4, r4).wait_recv()
        q_col = [msg2[1], msg2[2]]
        for i in plane[::-1]:
            q_col = [q_col[j] + in3[i, j] for j in range(2)]

        @pl.when(jnp.logical_not(is_hub))
        def _():
            many(in5, s7, r7).wait_recv()
            total = in5[0]
            for i in range(1, n_row):
                total = total + in5[i]
            qbuf[0] = total

        @pl.when(is_hub)
        def _():
            qbuf[0] = jnp.where(row == 2 * col, q_col[0], q_col[1])

        for j in range(2):
            @pl.when(row != 2 * col + j)
            def _():
                many(in4.at[pl.ds(j * n_col, n_col)], s6, r6.at[j]).wait_recv()
                total = in4[j * n_col]
                for i in range(1, n_col):
                    total = total + in4[j * n_col + i]
                qbuf[1 + j] = total

            @pl.when(row == 2 * col + j)
            def _():
                qbuf[1 + j] = q_row

        q_tiles = (q_row + qbuf[0], q_col[0] + qbuf[1], q_col[1] + qbuf[2])
        t_tiles = tuple(q_tiles[i] / zbuf[i, 9:18, :] - z_tiles[i] for i in range(3))
        at_hub_only = jnp.where(is_hub, zbuf[0, 9:18, :], 0.0)
        own[0:1, :] = col_sum(at_hub_only * z_tiles[0] * z_tiles[0])
        own[1:2, :] = col_sum(at_hub_only * z_tiles[0] * t_tiles[0])
        own[2:3, :] = col_sum(at_hub_only * t_tiles[0] * t_tiles[0])

        m0, m1, b, y = pushed(t_tiles)
        for i in range(3):
            yvec[6 + i] = y[i]
        square = m0 * m0 + m1 * m1
        form = -0.5 * (b[0] * y[0] + b[1] * y[1] + b[2] * y[2])
        for at in range(0, dense, 8):
            form = form + square[at : at + 8]
        t = t_tiles[0]
        form = form + damp[0:8] * t[0:8] * t[0:8]
        own[3:4, :] = col_sum(form) + damp[8:9] * t[8:9] * t[8:9]

        quarter = lax.broadcasted_iota(jnp.int32, (4, LANES), 1) // 32
        which = lax.broadcasted_iota(jnp.int32, (4, LANES), 0)
        four = own[...]
        four = four + pltpu.roll(four, 64, axis=1)
        four = four + pltpu.roll(four, 32, axis=1)
        stot[0:1, :] = col_sum(jnp.where(quarter == which, four, 0.0))

        def total_copy(i, j):
            slot = i * n_col + j
            return pltpu.make_async_remote_copy(
                src_ref=stot.at[pl.ds(0, 1)],
                dst_ref=stot.at[pl.ds(slot, 1)],
                send_sem=s5,
                recv_sem=r5,
                device_id=(up(i), over(j)),
                device_id_type=MESH,
            )

        def total_wait():
            return pltpu.make_async_remote_copy(
                src_ref=stot.at[pl.ds(1, n_row * n_col - 1)],
                dst_ref=stot.at[pl.ds(1, n_row * n_col - 1)],
                send_sem=s5,
                recv_sem=r5,
                device_id=(row, over(1)),
                device_id_type=MESH,
            )

        far = sorted(
            [(i, j) for i in range(n_row) for j in range(n_col) if i or j],
            key=lambda ij: -(apart(ij[0]) + min(ij[1], n_col - ij[1]) / 2),
        )
        for i, j in far:
            total_copy(i, j).start()

        def chosen(tile, first_entry, count):
            entry = lax.broadcasted_iota(jnp.int32, (8, LANES), 1) + first_entry
            level = lax.broadcasted_iota(jnp.int32, (8, LANES), 0)
            entry = jnp.minimum(entry, 143)
            cam = entry // 9
            rest = entry - 9 * cam
            at = cam + 16 * col
            low = jnp.where(rest == level, lane_gather(tile[0:8], at), 0.0)
            high = lane_gather(jnp.broadcast_to(tile[8:9], (8, LANES)), at)
            return col_sum(low + jnp.where((rest == 8) & (level == 0), high, 0.0))[:, :count]

        z_own = jnp.concatenate([chosen(z_tiles[0], 0, 128), chosen(z_tiles[0], 128, 16)], axis=1)
        t_own = jnp.concatenate([chosen(t_tiles[0], 0, 128), chosen(t_tiles[0], 128, 16)], axis=1)

        sent_to_hubs(msg1, s1, r1)
        spread_done(in1, s2, r2)

        many(in2.at[pl.ds(1, n_col - 1)], s3, r3).wait_send()
        many(in3.at[pl.ds(1, n_row - 1)], s4, r4).wait_send()
        many(in5.at[pl.ds(1, n_row - 1)], s6, r7).wait_send()
        many(in4.at[pl.ds(2, 2 * n_col - 2)], s7, r7).wait_send()

        total_wait().wait_recv()
        total = jnp.where(quarter == which, col_sum(stot[...]), 0.0)
        scalars = jnp.sum(total, axis=1, keepdims=True)
        rz, e, f, h = (scalars[i : i + 1] for i in range(4))
        pq = rz + e
        per_pq, per_rz = 1.0 / pq, 1.0 / rz
        a0 = rz * per_pq
        new = a0 * ((rz * f - e * e) * per_pq)
        g = e * per_pq + new * per_rz
        curve = g * g * pq - 2.0 * g * a0 * (e + f) + a0 * a0 * h
        a1 = new / curve
        big_a = a0 + a1 * g
        big_b = -a1 * a0
        cam_ref[...] = big_a * z_own + big_b * t_own
        for b in range(3):
            land = -(yvec[b] + big_a * yvec[3 + b] + big_b * yvec[6 + b])
            land_ref[b] = land[0:n_cl]
        total_wait().wait_send()

    return kernel


def write_out(cam_ref, land_ref, cam_out, land_out, sem):
    copies = (
        pltpu.make_async_copy(cam_ref, cam_out, sem.at[0]),
        pltpu.make_async_copy(land_ref, land_out, sem.at[1]),
    )
    for copy in copies:
        copy.start()
    for copy in copies:
        copy.wait()


def per_device(cam_jac, land_jac, resid, obs_cam, obs_land, pairs, cam_damp):
    n_row = lax.axis_size("row")
    n_col = lax.axis_size("col")
    n_cl, _, n_obs = cam_jac.shape
    shard = cam_damp.shape[0]
    f32 = jnp.float32
    slots = n_row + n_col
    tiles = n_obs // LANES
    dense = n_cl * tiles
    vmem = pl.BlockSpec(memory_space=pltpu.VMEM)
    dma = pltpu.SemaphoreType.DMA

    def entries_first(x):
        return (
            x.reshape(n_cl, -1, tiles, LANES).transpose(1, 2, 0, 3).reshape(-1, LANES)
        )

    cam, land = pl.pallas_call(
        make_kernel(n_row, n_col, n_cl, n_obs),
        out_shape=(
            jax.ShapeDtypeStruct((1, shard), f32),
            jax.ShapeDtypeStruct((3, n_cl, LANES), f32),
        ),
        in_specs=[pl.BlockSpec(memory_space=pltpu.HBM)] * 7,
        out_specs=(vmem, vmem),
        scratch_shapes=[
            pltpu.SMEM((2, n_cl), jnp.int32),
            pltpu.VMEM((18 * dense, LANES), f32),
            pltpu.VMEM((6 * dense, LANES), f32),
            pltpu.VMEM((2 * dense, LANES), f32),
            pltpu.VMEM((dense, LANES), jnp.int32),
            pltpu.VMEM((dense, LANES), jnp.int32),
            pltpu.VMEM((1, shard), f32),
            dma((7,)),
            pltpu.VMEM((n_cl, LANES, n_obs), jnp.bfloat16),
            pltpu.VMEM((n_cl, LANES, n_obs), jnp.bfloat16),
            pltpu.VMEM((32 * dense, LANES), f32),
            pltpu.VMEM((24 * dense, LANES), f32),
            pltpu.VMEM((32 * dense, LANES), f32),
            pltpu.VMEM((16 * dense, LANES), f32),
            pltpu.VMEM((2 * n_cl * 32, LANES), f32),
            pltpu.VMEM((2 * n_cl * 16, LANES), f32),
            pltpu.VMEM((6, 8, LANES), f32),
            pltpu.VMEM((9, 8, LANES), f32),
            pltpu.VMEM((3, 18, LANES), f32),
            pltpu.VMEM((3, 9, LANES), f32),
            pltpu.VMEM((slots, 18, LANES), f32),
            pltpu.VMEM((3, 18, LANES), f32),
            pltpu.VMEM((n_col, 9, LANES), f32),
            pltpu.VMEM((n_row, 2, 9, LANES), f32),
            pltpu.VMEM((2 * n_col, 9, LANES), f32),
            pltpu.VMEM((n_row, 9, LANES), f32),
            pltpu.VMEM((3, 9, LANES), f32),
            pltpu.VMEM((4, LANES), f32),
            pltpu.VMEM((n_row * n_col, LANES), f32),
            dma, dma((2,)),
            dma, dma((3,)),
            dma, dma,
            dma, dma,
            dma, dma,
            dma, dma((2,)),
            dma, dma,
        ],
        compiler_params=pltpu.CompilerParams(collective_id=0, has_side_effects=True, vmem_limit_bytes=VMEM),
        name="schur_step",
    )(
        *(
            pltpu.with_memory_space_constraint(x, pltpu.HBM)
            for x in (
        pairs.T,
        entries_first(cam_jac),
        entries_first(land_jac),
        resid.reshape(n_cl, 2, tiles, LANES).transpose(0, 2, 1, 3).reshape(-1, LANES),
        obs_cam.reshape(n_cl, tiles, LANES).transpose(1, 0, 2).reshape(-1, LANES),
        obs_land.reshape(n_cl, tiles, LANES).transpose(1, 0, 2).reshape(-1, LANES),
        cam_damp.reshape(1, shard),
            )
        )
    )
    cam, land = pl.pallas_call(
        write_out,
        out_shape=(
            jax.ShapeDtypeStruct((1, shard), f32),
            jax.ShapeDtypeStruct((3, n_cl, LANES), f32),
        ),
        in_specs=[vmem] * 2,
        out_specs=[pl.BlockSpec(memory_space=pltpu.HBM)] * 2,
        scratch_shapes=[dma((2,))],
        compiler_params=pltpu.CompilerParams(vmem_limit_bytes=1 << 20),
        name="write_out",
    )(cam, land)
    return cam.reshape(shard), land.transpose(1, 0, 2)


def solution(mesh):
    in_specs = (
        P(("row", "col"), None, None),
        P(("row", "col"), None, None),
        P(("row", "col"), None, None),
        P(("row", "col"), None),
        P(("row", "col"), None),
        P(("row", "col"), None),
        P(("row", "col")),
    )
    out_specs = (P(("row", "col")), P(("row", "col"), None, None))
    return jax.shard_map(
        per_device, mesh=mesh, in_specs=in_specs, out_specs=out_specs, check_vma=False
    )
```
